32 devices in a mesh: dp: 8 (over z, x), seq: 4 (over y, core).
Axes of the slice: x: 2, y: 2, z: 4, core: 2. Of those that a mesh axis runs over, the one named last changes fastest.
Arguments:
- stream_in: bfloat16 [16, 1024, 768], P('dp', 'seq'), may hold values from -6 to 6
- chosen: int32 [16, 256], P('dp', 'seq'), may hold values from 0 to 255, as said below
- counts: int32 [16, 4], P('dp'), may hold values from 16 to 64, as said below
- route_w: bfloat16 [768], replicated, may hold values from -0.21875 to 0.21875
- gain_a1: bfloat16 [768], replicated, may hold values from 0.5 to 1.5
- qkv_a: bfloat16 [768, 2304], replicated, may hold values from -0.21875 to 0.21875
- out_a: bfloat16 [768, 768], replicated, may hold values from -1.25 to 1.25
- gain_a2: bfloat16 [768], replicated, may hold values from 0.5 to 1.5
- up_a: bfloat16 [768, 3072], replicated, may hold values from -0.21875 to 0.21875
- down_a: bfloat16 [3072, 768], replicated, may hold values from -0.109375 to 0.109375
- gain_b1: bfloat16 [768], replicated, may hold values from 0.5 to 1.5
- qkv_b: bfloat16 [768, 2304], replicated, may hold values from -0.21875 to 0.21875
- out_b: bfloat16 [768, 768], replicated, may hold values from -1.75 to 1.75
- gain_b2: bfloat16 [768], replicated, may hold values from 0.5 to 1.5
- up_b: bfloat16 [768, 3072], replicated, may hold values from -0.21875 to 0.21875
- down_b: bfloat16 [3072, 768], replicated, may hold values from -0.109375 to 0.109375
- cotangent: bfloat16 [16, 1024, 768], P('dp', 'seq'), may hold values from -6 to 6
Outputs:
- output: bfloat16 [16, 1024, 768], P('dp', 'seq')
- grad_input: float32 [16, 1024, 768], P('dp', 'seq')
- grad_route: float32 [768], P('dp')
- grad_gain_a1: float32 [768], P('dp')
- grad_qkv_a: float32 [768, 2304], P('dp')
- grad_out_a: float32 [768, 768], P('dp')
- grad_gain_a2: float32 [768], P('dp')
- grad_up_a: float32 [768, 3072], P('dp')
- grad_down_a: float32 [3072, 768], P('dp')
- grad_gain_b1: float32 [768], P('dp')
- grad_qkv_b: float32 [768, 2304], P('dp')
- grad_out_b: float32 [768, 768], P('dp')
- grad_gain_b2: float32 [768], P('dp')
- grad_up_b: float32 [768, 3072], P('dp')
- grad_down_b: float32 [3072, 768], P('dp')
The draws below stay inside these ranges and needn't reach their ends.
Inputs may be any that keep to these rules, and one draw needn't show every extreme that they name: `chosen`: in each row, the slots of one device hold in their first counts entries distinct positions in increasing order; the other slots hold 0. `counts`: some device of some sequence holds exactly 64 routed tokens.
All inputs are finite; a program needn't handle non-finite values.
Results may differ from the reference program's by a relative error of at most 0.023.
Values may be sent and summed in bfloat16 or wider, within the bound.
No kernel may reach another device: no remote copies, remote signals or barrier semaphores. Data moves between devices by JAX's collectives and lax.ppermute only.
A program may use at most 192 MiB of HBM per device.

```python
import jax
import jax.numpy as jnp
from jax import lax

D = 768
HEADS = 12
HEAD_DIM = 64
FF = 3072
SHARD_TOK = 256
CAP = 64
LEN = 1024
SEQS = 16
N_SEQ = 4


def route_tables(key):
    base_key = jax.random.fold_in(key, 17)
    first_key, tail_key, size_key, spot_key, order_key = jax.random.split(base_key, 5)
    shape_two = (SEQS, N_SEQ)
    lower_load = jax.random.randint(first_key, shape_two, CAP // 4, CAP // 2 + 1)
    extra_load = jax.random.randint(tail_key, shape_two, 0, 2) * jax.random.randint(size_key, shape_two, 0, CAP // 2 + 1)
    load_counts = jnp.minimum(lower_load + extra_load, CAP)
    spot_at = jax.random.randint(spot_key, (), 0, SEQS * N_SEQ)
    flat_ids = jnp.arange(SEQS * N_SEQ, dtype=jnp.int32).reshape(shape_two)
    load_counts = jnp.where(flat_ids == spot_at, CAP, load_counts).astype(jnp.int32)
    rank_keys = jax.random.randint(order_key, (SEQS, N_SEQ, SHARD_TOK), 0, 2 ** 19) * SHARD_TOK + jnp.arange(SHARD_TOK, dtype=jnp.int32)
    order_ids = jnp.argsort(rank_keys, axis=-1, stable=True)[..., :CAP].astype(jnp.int32)
    slot_ids = jnp.arange(CAP, dtype=jnp.int32)
    filled = slot_ids < load_counts[..., None]
    marked = jnp.where(filled, order_ids, SHARD_TOK + slot_ids)
    ordered = jnp.sort(marked, axis=-1)
    chosen_ids = jnp.where(ordered < SHARD_TOK, ordered, 0).reshape(SEQS, N_SEQ * CAP)
    return (chosen_ids.astype(jnp.int32), load_counts)


def draw_chosen(key, part):
    return route_tables(key)[0]


def draw_counts(key, part):
    return route_tables(key)[1]


def steps_of(own_key, extent, cuts, smallest, top_value):
    level, own = 1.0, jax.random.fold_in(own_key, 6)
    for axis_at, shards_of in cuts:
        draws = jnp.exp(jax.random.uniform(jax.random.fold_in(own, axis_at), (shards_of,), jnp.float32, smallest / len(cuts), top_value / len(cuts)))
        level = level * jnp.repeat(draws, extent[axis_at] // shards_of).reshape([-1 if axis == axis_at else 1 for axis in range(len(extent))])
    return level


def scatter_about(stream_key, extent, deviation, bound, pieces=(), kind=jnp.bfloat16):
    values = deviation * jax.random.normal(stream_key, extent, jnp.float32)
    if pieces:
        values = values * steps_of(stream_key, extent, pieces, -0.22, 0.18)
    return jnp.clip(values, -bound, bound).astype(kind)


def setup_inputs(seed: int = 0) -> dict:
    key_list = jax.random.split(jax.random.key(seed), 18)
    stream_in = scatter_about(key_list[0], (SEQS, LEN, D), 1.0, 6.0, ((0, 8), (1, 4)))
    chosen = draw_chosen(jax.random.fold_in(key_list[17], 71), 0)
    counts = draw_counts(jax.random.fold_in(key_list[17], 71), 0)
    route_w = scatter_about(key_list[3], (D,), D ** -0.5, 0.21875)
    gain_a1 = jnp.clip(1.0 + 0.1 * jax.random.normal(key_list[4], (D,), jnp.float32), 0.5, 1.5).astype(jnp.bfloat16)
    qkv_a = scatter_about(key_list[5], (D, 3 * D), D ** -0.5, 0.21875)
    out_a = scatter_about(key_list[6], (D, D), (D // 32) ** -0.5, 1.25)
    gain_a2 = jnp.clip(1.0 + 0.1 * jax.random.normal(key_list[7], (D,), jnp.float32), 0.5, 1.5).astype(jnp.bfloat16)
    up_a = scatter_about(key_list[8], (D, FF), D ** -0.5, 0.21875)
    down_a = scatter_about(key_list[9], (FF, D), FF ** -0.5, 0.109375)
    gain_b1 = jnp.clip(1.0 + 0.1 * jax.random.normal(key_list[10], (D,), jnp.float32), 0.5, 1.5).astype(jnp.bfloat16)
    qkv_b = scatter_about(key_list[11], (D, 3 * D), D ** -0.5, 0.21875)
    out_b = scatter_about(key_list[12], (D, D), (D // 64) ** -0.5, 1.75)
    gain_b2 = jnp.clip(1.0 + 0.1 * jax.random.normal(key_list[13], (D,), jnp.float32), 0.5, 1.5).astype(jnp.bfloat16)
    up_b = scatter_about(key_list[14], (D, FF), D ** -0.5, 0.21875)
    down_b = scatter_about(key_list[15], (FF, D), FF ** -0.5, 0.109375)
    cotangent = scatter_about(key_list[16], (SEQS, LEN, D), 1.0, 6.0, ((0, 8), (1, 4)))
    return {"stream_in": stream_in, "chosen": chosen, "counts": counts, "route_w": route_w, "gain_a1": gain_a1, "qkv_a": qkv_a, "out_a": out_a, "gain_a2": gain_a2, "up_a": up_a, "down_a": down_a, "gain_b1": gain_b1, "qkv_b": qkv_b, "out_b": out_b, "gain_b2": gain_b2, "up_b": up_b, "down_b": down_b, "cotangent": cotangent}


@jax.custom_vjp
def low(v):
    return lax.optimization_barrier(v.astype(jnp.bfloat16)).astype(jnp.float32)

@jax.custom_vjp
def low_back(v):
    return v

def low_keep(v):
    return (low(v), None)

def low_pass(kept, grad):
    return (grad,)

def back_keep(v):
    return (v, None)

def back_low(kept, grad):
    return (low(grad),)
low.defvjp(low_keep, low_pass)
low_back.defvjp(back_keep, back_low)
EXACT = lax.Precision.HIGHEST
EPSILON = 1e-06

def norm_rows(vector, gain_vec):
    return vector * lax.rsqrt(lax.optimization_barrier(jnp.mean(vector * vector, axis=-1, keepdims=True)) + EPSILON) * gain_vec

def matmul(left_side, weight):
    return jnp.dot(left_side, weight, precision=EXACT)

def attend(queries, key_rows, value_rows, visible):
    row_count = queries.shape[0]
    key_count = key_rows.shape[0]
    query_heads = queries.reshape(row_count, HEADS, HEAD_DIM)
    key_heads = key_rows.reshape(key_count, HEADS, HEAD_DIM)
    value_heads = value_rows.reshape(key_count, HEADS, HEAD_DIM)
    scores = jnp.einsum('qhd,khd->hqk', query_heads, key_heads, precision=EXACT) * HEAD_DIM ** (-0.5)
    scores = low_back(scores)
    scores = jnp.where(visible[None], scores, -1e+30)
    row_max = lax.optimization_barrier(jnp.max(scores, axis=-1, keepdims=True))
    exponent = jnp.exp(scores - row_max)
    probability = low(exponent / lax.optimization_barrier(jnp.sum(exponent, axis=-1, keepdims=True)))
    mixture = jnp.einsum('hqk,khd->qhd', probability, value_heads, precision=EXACT)
    return mixture.reshape(row_count, HEADS * HEAD_DIM)

def layer_pass(resid, router, visible, gain_one, w_qkv, w_out, gain_two, w_up, w_down):
    act_in = low(norm_rows(resid, gain_one))
    packed = matmul(act_in, w_qkv)
    queries = low_back(low(packed[:, :D]))
    key_rows = low_back(low(packed[:, D:2 * D]))
    value_rows = low_back(low(packed[:, 2 * D:]))
    mixture = low_back(low(attend(queries, key_rows, value_rows, visible)))
    attended = low_back(matmul(mixture, w_out))
    middle = resid + router[:, None] * attended
    ff_in = low(norm_rows(middle, gain_two))
    hidden = low_back(matmul(ff_in, w_up))
    activated = low(jax.nn.gelu(hidden))
    branch_out = low_back(matmul(activated, w_down))
    return middle + branch_out

def per_sequence(weight_set, item_set):
    seq_rows, seq_chosen, seq_counts = item_set
    route_f, ga1, qa, oa, ga2, ua, da, gb1, qb, ob, gb2, ub, db = weight_set
    slot_ids = jnp.arange(N_SEQ * CAP, dtype=jnp.int32)
    owner_ids = slot_ids // CAP
    place_ids = slot_ids % CAP
    live_slots = place_ids < seq_counts[owner_ids]
    row_ids = (owner_ids * SHARD_TOK + seq_chosen).astype(jnp.int32)
    picked = seq_rows[row_ids]
    router = jnp.dot(picked, route_f, precision=EXACT)
    same_owner = owner_ids[None, :] == owner_ids[:, None]
    seen = live_slots[None, :] & ((owner_ids[None, :] < owner_ids[:, None]) | same_owner & (place_ids[None, :] <= place_ids[:, None]))
    seen = seen | (slot_ids[None, :] == slot_ids[:, None])
    done_sel = layer_pass(picked, router, seen, ga1, qa, oa, ga2, ua, da)
    change = jnp.where(live_slots[:, None], done_sel - picked, 0.0)
    middle = seq_rows.at[row_ids].add(change)
    positions = jnp.arange(LEN, dtype=jnp.int32)
    causal = positions[None, :] <= positions[:, None]
    unit_gates = jnp.ones((LEN,), dtype=jnp.float32)
    return layer_pass(middle, unit_gates, causal, gb1, qb, ob, gb2, ub, db)

def reference(stream_in, chosen, counts, route_w, gain_a1, qkv_a, out_a, gain_a2, up_a, down_a, gain_b1, qkv_b, out_b, gain_b2, up_b, down_b, cotangent):
    weight_set = tuple((w.astype(jnp.float32) for w in (route_w, gain_a1, qkv_a, out_a, gain_a2, up_a, down_a, gain_b1, qkv_b, out_b, gain_b2, up_b, down_b)))
    checked = jax.checkpoint(per_sequence)

    def forward(rows_all, weights_all):
        return lax.map(lambda item_set: checked(weights_all, item_set), (rows_all, chosen, counts))
    result, pullback = jax.vjp(forward, stream_in.astype(jnp.float32), weight_set)
    grad_rows, grad_weights = pullback(cotangent.astype(jnp.float32))
    g_route, g_ga1, g_qa, g_oa, g_ga2, g_ua, g_da, g_gb1, g_qb, g_ob, g_gb2, g_ub, g_db = grad_weights
    return (result.astype(jnp.bfloat16), grad_rows, g_route, g_ga1, g_qa, g_oa, g_ga2, g_ua, g_da, g_gb1, g_qb, g_ob, g_gb2, g_ub, g_db)
```

```python
import jax
import jax.numpy as jnp
from jax import lax
from jax.experimental import pallas as pl
from jax.experimental.pallas import tpu as pltpu
from jax.sharding import PartitionSpec as P

HEADS = 12
HEAD_DIM = 64
EPSILON = 1e-06
EXACT = lax.Precision.HIGHEST
F32 = jnp.float32
BF16 = jnp.bfloat16
OWNERS = 4
LANES = 128
BLOCK = 256
VMEM_BYTES = 60 * 1024 * 1024

SMEM_SPEC = pl.BlockSpec(memory_space=pltpu.SMEM)
VMEM_SPEC = pl.BlockSpec(memory_space=pltpu.VMEM)
NT = (((1,), (1,)), ((), ()))
TN = (((0,), (0,)), ((), ()))


def dot(left, right, dims=(((1,), (0,)), ((), ()))):
    return lax.dot_general(left, right, dims, preferred_element_type=F32)


def cost(flops, moved, exps=0):
    return pl.CostEstimate(flops=int(flops), bytes_accessed=int(moved), transcendentals=int(exps))


def project_kernel(place, x_ref, gain_ref, w_ref, act_ref, *outs):
    width = x_ref.shape[-1]
    half = width // 2
    for i in range(2):
        x = x_ref[i].astype(F32)
        scale = lax.rsqrt(jnp.mean(x * x, axis=-1, keepdims=True) + EPSILON)
        act_ref[i] = (x * scale * gain_ref[...].astype(F32)).astype(BF16)
    for r in (3, 2, 1, 0):
        act = act_ref[place[0] ^ (r >> 1)]
        at = (place[1] ^ (r & 1)) * half
        for part in range(3):
            columns = pl.ds(pl.multiple_of(part * width + at, LANES), half)
            outs[r][part] = dot(act, w_ref[:, columns]).astype(BF16)


def project_pieces(place, x, gain, weight):
    seqs, rows, width = x.shape
    piece = jax.ShapeDtypeStruct((3, rows, width // 2), BF16)
    outs = pl.pallas_call(
        project_kernel,
        name="project_pieces",
        out_shape=[jax.ShapeDtypeStruct(x.shape, BF16)] + [piece] * OWNERS,
        in_specs=[SMEM_SPEC] + [VMEM_SPEC] * 3,
        out_specs=[VMEM_SPEC] * (1 + OWNERS),
        compiler_params=pltpu.CompilerParams(vmem_limit_bytes=VMEM_BYTES),
        cost_estimate=cost(
            2 * seqs * rows * width * 3 * width, 6 * width * width + 12 * seqs * rows * width
        ),
    )(place, x, gain.reshape(1, width), weight)
    return outs[0], outs[1:]


def lane_head(head):
    lanes = lax.broadcasted_iota(jnp.int32, (1, LANES), 1)
    return (lanes < HEAD_DIM) if head == 0 else (lanes >= HEAD_DIM)


def only_head(x, head):
    return jnp.where(lane_head(head), x, jnp.zeros_like(x))


def slot_matrix(chosen_ref, counts, owner, rows):
    slots = chosen_ref.shape[1]
    spots = chosen_ref[pl.ds(owner, 1), :]
    row_ids = lax.broadcasted_iota(jnp.int32, (rows, slots), 0)
    slot_ids = lax.broadcasted_iota(jnp.int32, (rows, slots), 1)
    return jnp.where((row_ids == spots) & (slot_ids < counts[owner]), 1.0, 0.0)


def diagonal_mask(counts, query_axis, rows, routed):
    shape = (BLOCK, BLOCK)
    queries = lax.broadcasted_iota(jnp.int32, shape, query_axis)
    keys = lax.broadcasted_iota(jnp.int32, shape, 1 - query_axis)
    if not routed:
        return keys <= queries
    owner = keys // rows
    load = jnp.where(
        owner == 0,
        counts[0],
        jnp.where(owner == 1, counts[1], jnp.where(owner == 2, counts[2], counts[3])),
    )
    live = (keys - owner * rows) < load
    return (keys == queries) | ((keys < queries) & live)


def attend_kernel(rows, routed, place, counts, *refs):
    if routed:
        base, refs = refs[:OWNERS], refs[OWNERS:]
    else:
        chosen_ref, base, slot_in = refs[0], refs[1 : 1 + OWNERS], refs[1 + OWNERS : 1 + 2 * OWNERS]
        refs = refs[1 + 2 * OWNERS :]
    outs, (merged, stats, mixed) = refs[:OWNERS], refs[OWNERS:]
    me = 2 * place[0] + place[1]
    blocks = OWNERS * rows // BLOCK
    for r in range(OWNERS):
        owner = me ^ r
        at = pl.ds(pl.multiple_of(owner * rows, rows), rows)
        if routed:
            for part in range(3):
                merged[part, at, :] = base[r][part]
        else:
            spots = slot_matrix(chosen_ref, counts, owner, rows)
            covered = jnp.max(spots, axis=1, keepdims=True) > 0.5
            spots = spots.astype(BF16)
            for part in range(3):
                placed = dot(spots, slot_in[r][part])
                merged[part, at, :] = jnp.where(
                    covered, placed, base[r][part].astype(F32)
                ).astype(BF16)
    visible = diagonal_mask(counts, 0, rows, routed)
    for a in range(blocks):
        queries = merged[0, a * BLOCK : (a + 1) * BLOCK, :] * jnp.asarray(HEAD_DIM**-0.5, BF16)
        mixture = jnp.zeros((BLOCK, LANES), F32)
        stat = jnp.zeros((BLOCK, LANES), F32)
        for head in range(2):
            own = only_head(queries, head)
            scores = []
            for b in range(a + 1):
                keys = merged[1, b * BLOCK : (b + 1) * BLOCK, :]
                found = dot(own, keys, NT)
                scores.append(jnp.where(visible, found, -1e30) if b == a else found)
            top = scores[0]
            for found in scores[1:]:
                top = jnp.maximum(top, found)
            top = jnp.max(top, axis=1, keepdims=True)
            total = jnp.zeros((BLOCK, BLOCK), F32)
            part = jnp.zeros((BLOCK, LANES), F32)
            for b in range(a + 1):
                weight = jnp.exp(scores[b] - top)
                total = total + weight
                values = only_head(merged[2, b * BLOCK : (b + 1) * BLOCK, :], head)
                part = part + dot(weight.astype(BF16), values)
            total = jnp.sum(total, axis=1, keepdims=True)
            mixture = mixture + part * (1.0 / total)
            lane = lax.broadcasted_iota(jnp.int32, (1, LANES), 1)
            stat = jnp.where(lane == head, top + jnp.log(total), stat)
        mixed[a * BLOCK : (a + 1) * BLOCK, :] = mixture.astype(BF16)
        stats[0, :, a * BLOCK : (a + 1) * BLOCK] = stat.T[:8, :]
    for r in range(OWNERS):
        at = pl.ds(pl.multiple_of((me ^ r) * rows, rows), rows)
        outs[r][...] = mixed[at, :]


def attend(place, counts, base, chosen=None, slots=None):
    routed = slots is None
    _, rows, half = base[0].shape
    pairs = half // LANES
    length = OWNERS * rows
    inputs = [place, counts]
    specs = [SMEM_SPEC, SMEM_SPEC]
    if not routed:
        inputs.append(chosen)
        specs.append(VMEM_SPEC)
    for group in (base, slots):
        if group is not None:
            inputs += list(group)
            specs += [
                pl.BlockSpec((3, group[0].shape[1], LANES), lambda h: (0, 0, h))
            ] * OWNERS
    blocks = length // BLOCK
    work = blocks * (blocks + 1) // 2 * BLOCK * BLOCK * 2 * pairs
    outs = pl.pallas_call(
        lambda *refs: attend_kernel(rows, routed, *refs),
        name="attend_routed" if routed else "attend_dense",
        grid=(pairs,),
        out_shape=[jax.ShapeDtypeStruct((rows, half), BF16)] * OWNERS
        + [
            jax.ShapeDtypeStruct((3, length, half), BF16),
            jax.ShapeDtypeStruct((pairs, 8, length), F32),
        ],
        in_specs=specs,
        out_specs=[pl.BlockSpec((rows, LANES), lambda h: (0, h))] * OWNERS
        + [
            pl.BlockSpec((3, length, LANES), lambda h: (0, 0, h)),
            pl.BlockSpec((1, 8, length), lambda h: (h, 0, 0)),
        ],
        scratch_shapes=[pltpu.VMEM((length, LANES), BF16)],
        compiler_params=pltpu.CompilerParams(vmem_limit_bytes=VMEM_BYTES),
        cost_estimate=cost(16 * HEAD_DIM * work, 16 * length * half, work),
    )(*inputs)
    return outs[:OWNERS], outs[OWNERS], outs[OWNERS + 1]


def attend_back_kernel(rows, routed, place, counts, *refs):
    if not routed:
        chosen_ref, refs = refs[0], refs[1:]
    merged, stats, grads = refs[0], refs[1], refs[2 : 2 + OWNERS]
    outs, refs = refs[2 + OWNERS : 2 + 2 * OWNERS], refs[2 + 2 * OWNERS :]
    if not routed:
        slot_outs, refs = refs[:OWNERS], refs[OWNERS:]
    incoming, grad_q, grad_k, grad_v = refs
    me = 2 * place[0] + place[1]
    blocks = OWNERS * rows // BLOCK
    for r in range(OWNERS):
        at = pl.ds(pl.multiple_of((me ^ r) * rows, rows), rows)
        incoming[at, :] = grads[r][...]
    for ref in (grad_q, grad_k, grad_v):
        ref[...] = jnp.zeros_like(ref)
    visible = diagonal_mask(counts, 1, rows, routed)
    for a in range(blocks):
        span = slice(a * BLOCK, (a + 1) * BLOCK)
        queries = merged[0, span, :] * jnp.asarray(HEAD_DIM**-0.5, BF16)
        grad_mix = incoming[span, :]
        grad_query = jnp.zeros((BLOCK, LANES), F32)
        for head in range(2):
            own_q = only_head(queries, head)
            own_g = only_head(grad_mix, head)
            level = stats[0, head : head + 1, span]
            probs, grad_probs = [], []
            inner = jnp.zeros((1, BLOCK), F32)
            for b in range(a + 1):
                keys_at = slice(b * BLOCK, (b + 1) * BLOCK)
                prob = jnp.exp(dot(merged[1, keys_at, :], own_q, NT) - level)
                if b == a:
                    prob = jnp.where(visible, prob, 0.0)
                grad_prob = dot(merged[2, keys_at, :], own_g, NT)
                grad_v[keys_at, :] += dot(prob.astype(BF16), own_g)
                inner = inner + jnp.sum(prob * grad_prob, axis=0, keepdims=True)
                probs.append(prob)
                grad_probs.append(grad_prob)
            for b in range(a + 1):
                keys_at = slice(b * BLOCK, (b + 1) * BLOCK)
                grad_score = (probs[b] * (grad_probs[b] - inner)).astype(BF16)
                grad_k[keys_at, :] += dot(grad_score, own_q)
                own_k = only_head(merged[1, keys_at, :], head)
                grad_query = grad_query + dot(grad_score, own_k, TN)
        grad_q[span, :] = grad_query * HEAD_DIM**-0.5
    for r in range(OWNERS):
        owner = me ^ r
        at = pl.ds(pl.multiple_of(owner * rows, rows), rows)
        if not routed:
            spots = slot_matrix(chosen_ref, counts, owner, rows).astype(BF16)
        for part, ref in enumerate((grad_q, grad_k, grad_v)):
            found = ref[at, :].astype(BF16)
            outs[r][part] = found
            if not routed:
                slot_outs[r][part] = dot(spots, found, TN).astype(BF16)


def attend_back(place, counts, merged, stats, grads, chosen=None):
    routed = chosen is None
    rows, half = grads[0].shape
    pairs = half // LANES
    length = OWNERS * rows
    inputs = [place, counts]
    specs = [SMEM_SPEC, SMEM_SPEC]
    shapes = [jax.ShapeDtypeStruct((3, rows, half), BF16)] * OWNERS
    out_specs = [pl.BlockSpec((3, rows, LANES), lambda h: (0, 0, h))] * OWNERS
    if not routed:
        inputs.append(chosen)
        specs.append(VMEM_SPEC)
        slots = chosen.shape[1]
        shapes += [jax.ShapeDtypeStruct((3, slots, half), BF16)] * OWNERS
        out_specs += [pl.BlockSpec((3, slots, LANES), lambda h: (0, 0, h))] * OWNERS
    inputs += [merged, stats] + list(grads)
    specs += [
        pl.BlockSpec((3, length, LANES), lambda h: (0, 0, h)),
        pl.BlockSpec((1, 8, length), lambda h: (h, 0, 0)),
    ] + [pl.BlockSpec((rows, LANES), lambda h: (0, h))] * OWNERS
    blocks = length // BLOCK
    work = blocks * (blocks + 1) // 2 * BLOCK * BLOCK * 2 * pairs
    outs = pl.pallas_call(
        lambda *refs: attend_back_kernel(rows, routed, *refs),
        name="attend_routed_back" if routed else "attend_dense_back",
        grid=(pairs,),
        out_shape=shapes,
        in_specs=specs,
        out_specs=out_specs,
        scratch_shapes=[pltpu.VMEM((length, LANES), BF16)]
        + [pltpu.VMEM((length, LANES), F32)] * 3,
        compiler_params=pltpu.CompilerParams(vmem_limit_bytes=VMEM_BYTES),
        cost_estimate=cost(40 * HEAD_DIM * work, 16 * length * half, work),
    )(*inputs)
    return outs[:OWNERS], outs[OWNERS:]


def bit_reverse(number, bits):
    found = 0
    for k in range(bits):
        found = found | (((number >> k) & 1) << (bits - 1 - k))
    return found


def store_slabs(ref, found, first, slab_rows, at, place, bits):
    for d in range(found.shape[0] // slab_rows):
        spot = bit_reverse(first + d, bits) ^ place[2]
        ref[pl.ds(spot, 1), at : at + slab_rows, :] = found[
            d * slab_rows : (d + 1) * slab_rows
        ].astype(BF16)[None]


def feed_grad_kernel(bits, place, ff_ref, gh_ref, gel_ref, gff_ref, send_ref, own_ref):
    step, kind, tile = pl.program_id(0), pl.program_id(1), pl.program_id(2)
    width = ff_ref.shape[1]
    slabs = 1 << bits
    narrow, wide = width // slabs, OWNERS * width // slabs
    for core_step, ref in ((0, send_ref), (1, own_ref)):
        for t in range(OWNERS):

            @pl.when((step == core_step) & (kind == 0) & (tile == t))
            def _():
                found = dot(ff_ref[...], gh_ref[...], TN)
                store_slabs(ref, found, 0, narrow, t * narrow, place, bits)

            @pl.when((step == core_step) & (kind == 1) & (tile == t))
            def _():
                found = dot(gel_ref[...], gff_ref[...], TN)
                store_slabs(
                    ref, found, t * slabs // OWNERS, wide, OWNERS * narrow, place, bits
                )


def feed_grad(place, bits, ff_in, grad_hidden, activated, grad_ff):
    tokens, width = ff_in.shape
    half = width // 2
    slabs = 1 << bits
    rows = 2 * OWNERS * width // slabs

    def half_of(step, place_ref):
        return place_ref[1] ^ (1 - step)

    return pl.pallas_call(
        lambda *refs: feed_grad_kernel(bits, *refs),
        name="feed_grad",
        grid_spec=pltpu.PrefetchScalarGridSpec(
            num_scalar_prefetch=1,
            grid=(2, 2, OWNERS),
            in_specs=[
                pl.BlockSpec((tokens, width), lambda s, k, t, p: (0, 0)),
                pl.BlockSpec(
                    (tokens, half),
                    lambda s, k, t, p: (
                        0,
                        half_of(s, p) * OWNERS + jnp.where(k == 0, t, OWNERS - 1),
                    ),
                ),
                pl.BlockSpec((tokens, width), lambda s, k, t, p: (0, jnp.where(k == 0, 0, t))),
                pl.BlockSpec((tokens, half), lambda s, k, t, p: (0, half_of(s, p))),
            ],
            out_specs=[pl.BlockSpec((slabs, rows, half), lambda s, k, t, p: (0, 0, 0))] * 2,
        ),
        out_shape=[jax.ShapeDtypeStruct((slabs, rows, half), BF16)] * 2,
        compiler_params=pltpu.CompilerParams(vmem_limit_bytes=VMEM_BYTES),
        cost_estimate=cost(
            16 * tokens * width * width, 16 * width * width + 20 * tokens * width
        ),
    )(place, ff_in, grad_hidden, activated, grad_ff)


def mix_grad_kernel(bits, place, act_ref, p0, p1, p2, p3, mix_ref, gatt_ref, send_ref, own_ref):
    width = act_ref.shape[-1]
    half = width // 2
    narrow = width // (1 << bits)
    pieces = (p0, p1, p2, p3)
    for other, ref in ((1, send_ref), (0, own_ref)):
        for part in range(3):
            found = dot(act_ref[place[0]], pieces[other][part], TN)
            found = found + dot(act_ref[1 - place[0]], pieces[2 + other][part], TN)
            store_slabs(ref, found, 0, narrow, part * narrow, place, bits)
        columns = pl.ds(pl.multiple_of((place[1] ^ other) * half, LANES), half)
        found = dot(mix_ref[0], gatt_ref[0, :, columns], TN)
        found = found + dot(mix_ref[1], gatt_ref[1, :, columns], TN)
        store_slabs(ref, found, 0, narrow, 3 * narrow, place, bits)


def mix_grad(place, bits, act, pieces, mixture, grad_attended):
    seqs, rows, width = act.shape
    half = width // 2
    slabs = 1 << bits
    shape = jax.ShapeDtypeStruct((slabs, OWNERS * width // slabs, half), BF16)
    return pl.pallas_call(
        lambda *refs: mix_grad_kernel(bits, *refs),
        name="mix_grad",
        in_specs=[SMEM_SPEC] + [VMEM_SPEC] * 7,
        out_specs=[VMEM_SPEC] * 2,
        out_shape=[shape] * 2,
        compiler_params=pltpu.CompilerParams(vmem_limit_bytes=VMEM_BYTES),
        cost_estimate=cost(
            8 * seqs * rows * width * width, 8 * width * width + 12 * seqs * rows * width
        ),
    )(place, act, *pieces, mixture, grad_attended)


def swap(x, axis, bit):
    size = lax.axis_size(axis)
    return lax.ppermute(x, axis, [(i, i ^ bit) for i in range(size)])


def exchange(pieces):
    return [pieces[0]] + [swap(pieces[r], "seq", r) for r in range(1, OWNERS)]


def add_low(a, b):
    return (a.astype(F32) + b.astype(F32)).astype(BF16)


def reduce_group(send, own, bits):
    current = add_low(own, swap(send, "seq", 1))
    for k in range(bits):
        n = current.shape[0] // 2
        current = add_low(current[:n], swap(current[n:], "dp", 1 << k))
    current = add_low(current, swap(current, "seq", 2))
    return current[0], swap(current, "seq", 1)[0]


def both_halves(own, other, first):
    return jnp.concatenate(
        [jnp.where(first, own, other), jnp.where(first, other, own)], axis=-1
    )


def assemble(pieces, y_first, core_first):
    near = both_halves(pieces[0], pieces[1], core_first)
    far = both_halves(pieces[2], pieces[3], core_first)
    return jnp.stack([jnp.where(y_first, near, far), jnp.where(y_first, far, near)])


def assemble_packed(pieces, y_first, core_first):
    found = assemble(pieces, y_first, core_first)
    return jnp.concatenate([found[:, 0], found[:, 1], found[:, 2]], axis=-1)


def split_pieces(x, place):
    half = x.shape[-1] // 2
    found = []
    for r in range(OWNERS):
        rows = lax.dynamic_index_in_dim(x, place[0] ^ (r >> 1), 0, keepdims=False)
        found.append(lax.dynamic_slice_in_dim(rows, (place[1] ^ (r & 1)) * half, half, axis=1))
    return found


def norm_rows(vector, gain_vec):
    return (
        vector * lax.rsqrt(jnp.mean(vector * vector, axis=-1, keepdims=True) + EPSILON) * gain_vec
    )


def project(left_side, weight):
    return jnp.einsum("bnd,de->bne", left_side, weight, preferred_element_type=F32)


def project_back(gradient, weight):
    return jnp.einsum("bne,de->bnd", gradient, weight, preferred_element_type=F32)


def feed_forward(resid, router, mixture, w_out, gain_two, w_up, w_down):
    attended = project(mixture, w_out)
    middle = resid + attended if router is None else resid + router[..., None] * attended
    ff_in = norm_rows(middle, gain_two.astype(F32)).astype(BF16)
    hidden = project(ff_in, w_up)
    activated = jax.nn.gelu(hidden).astype(BF16)
    done = middle + project(activated, w_down)
    return done, (attended, middle, ff_in, hidden, activated)


def feed_backward(grad_done, router, w_out, gain_two, w_up, w_down, kept):
    attended, middle, ff_in, hidden, activated = kept
    grad_ff = grad_done.astype(BF16)
    grad_act = project_back(grad_ff, w_down)
    unused_value, gelu_pull = jax.vjp(jax.nn.gelu, hidden)
    grad_hidden = gelu_pull(grad_act)[0].astype(BF16)
    grad_ffin = project_back(grad_hidden, w_up)
    unused_norm, norm_pull = jax.vjp(norm_rows, middle, gain_two.astype(F32))
    grad_mid_norm, grad_gain_two = norm_pull(grad_ffin)
    grad_middle = grad_done + grad_mid_norm
    scaled = grad_middle if router is None else router[..., None] * grad_middle
    grad_attended = scaled.astype(BF16)
    grad_mixture = project_back(grad_attended, w_out).astype(BF16)
    return grad_ff, grad_hidden, grad_middle, grad_gain_two, grad_attended, grad_mixture


def norm_back(x, gain, grad_act_in):
    unused, pull = jax.vjp(norm_rows, x, gain.astype(F32))
    return pull(grad_act_in)


def per_device(
    stream_in,
    chosen,
    counts,
    route_w,
    gain_a1,
    qkv_a,
    out_a,
    gain_a2,
    up_a,
    down_a,
    gain_b1,
    qkv_b,
    out_b,
    gain_b2,
    up_b,
    down_b,
    cotangent,
):
    seqs, rows, width = stream_in.shape
    slots = chosen.shape[1]
    half = width // 2
    dp_size = lax.axis_size("dp")
    bits = dp_size.bit_length() - 1
    me = lax.axis_index("seq")
    y_at, core_at = me // 2, me % 2
    y_first, core_first = y_at == 0, core_at == 0
    place = jnp.stack(
        [y_at, core_at, bit_reverse(lax.axis_index("dp"), bits)]
    ).astype(jnp.int32)
    chosen_all = lax.all_gather(chosen, "seq", axis=0)
    chosen_mine = lax.dynamic_index_in_dim(chosen_all, y_at, 1, keepdims=False)
    counts_mine = lax.dynamic_index_in_dim(counts, y_at, 0, keepdims=False)
    own_load = lax.dynamic_index_in_dim(counts, me, 1, keepdims=False)
    live = jnp.arange(slots, dtype=jnp.int32)[None, :] < own_load[:, None]
    hits = chosen[:, :, None] == jnp.arange(rows, dtype=jnp.int32)
    gather = hits.astype(BF16)
    live_hits = (hits & live[..., None]).astype(F32)
    covered = jnp.any(hits & live[..., None], axis=1)[..., None]

    def scatter(values):
        return jnp.einsum("bcr,bcd->brd", live_hits, values, precision=EXACT)

    act_base, base = project_pieces(place, stream_in, gain_b1, qkv_b)

    picked = jnp.einsum("bcr,brd->bcd", gather, stream_in, preferred_element_type=F32)
    picked_low = picked.astype(BF16)
    router = jnp.einsum("bcd,d->bc", picked_low, route_w, preferred_element_type=F32)
    act_a, pieces = project_pieces(place, picked_low, gain_a1, qkv_a)
    mixed, merged_a, stats_a = attend(place, counts_mine, exchange(pieces))
    base = exchange(base)
    mixture_a = assemble(exchange(mixed), y_first, core_first)
    done_a, kept_a = feed_forward(picked, router, mixture_a, out_a, gain_a2, up_a, down_a)
    change = jnp.where(live[..., None], done_a - picked, 0.0)
    slot_mid = picked + change
    act_slot, slot_pieces = project_pieces(place, slot_mid, gain_b1, qkv_b)
    mixed, merged_b, stats_b = attend(
        place, counts_mine, base, chosen_mine, exchange(slot_pieces)
    )
    mixture_b = assemble(exchange(mixed), y_first, core_first)
    middle = stream_in.astype(F32) + scatter(change)
    done_b, kept_b = feed_forward(middle, None, mixture_b, out_b, gain_b2, up_b, down_b)

    grad_ff_b, grad_hidden_b, grad_mid_b, g_gb2, grad_att_b, grad_mix_b = feed_backward(
        cotangent.astype(F32), None, out_b, gain_b2, up_b, down_b, kept_b
    )
    grads = exchange(split_pieces(grad_mix_b, place))
    flat = lambda x: x.reshape(x.shape[0] * x.shape[1], x.shape[2])
    feed_b = reduce_group(
        *feed_grad(
            place, bits, flat(kept_b[2]), flat(grad_hidden_b), flat(kept_b[4]), flat(grad_ff_b)
        ),
        bits,
    )
    packed_b, packed_slot = attend_back(place, counts_mine, merged_b, stats_b, grads, chosen_mine)
    packed_slot = exchange(packed_slot)
    grad_packed_slot = assemble_packed(packed_slot, y_first, core_first)
    packed_b = exchange(packed_b)

    slot_grad, _ = norm_back(slot_mid, gain_b1, project_back(grad_packed_slot, qkv_b))
    mid_at_slot = jnp.einsum("bcr,brd->bcd", live_hits, grad_mid_b, precision=EXACT)
    grad_done = jnp.where(live[..., None], mid_at_slot + slot_grad, 0.0)
    grad_ff_a, grad_hidden_a, grad_mid_a, g_ga2, grad_att_a, grad_mix_a = feed_backward(
        grad_done, router, out_a, gain_a2, up_a, down_a, kept_a
    )
    grad_router = jnp.sum(kept_a[0] * grad_mid_a, axis=-1)
    grads = exchange(split_pieces(grad_mix_a, place))
    feed_a = reduce_group(
        *feed_grad(
            place, bits, flat(kept_a[2]), flat(grad_hidden_a), flat(kept_a[4]), flat(grad_ff_a)
        ),
        bits,
    )
    packed_a, _ = attend_back(place, counts_mine, merged_a, stats_a, grads)
    packed_a = exchange(packed_a)
    mix_a = reduce_group(*mix_grad(place, bits, act_a, packed_a, mixture_a, grad_att_a), bits)
    grad_packed_a = assemble_packed(packed_a, y_first, core_first)
    res_a, g_ga1 = norm_back(picked, gain_a1, project_back(grad_packed_a, qkv_a))
    grad_picked = (
        grad_mid_a + res_a + grad_router[..., None] * route_w.astype(F32) - grad_done
    )
    grad_route = jnp.einsum("bc,bcd->d", grad_router, picked, precision=EXACT)

    act_b = jnp.where(
        covered,
        jnp.einsum("bcr,bcd->brd", live_hits.astype(BF16), act_slot, preferred_element_type=F32),
        act_base.astype(F32),
    ).astype(BF16)
    mix_b = reduce_group(*mix_grad(place, bits, act_b, packed_b, mixture_b, grad_att_b), bits)
    grad_packed_b = assemble_packed(packed_b, y_first, core_first)
    res_b, g_gb1 = norm_back(middle, gain_b1, project_back(grad_packed_b, qkv_b))
    grad_input = grad_mid_b + res_b + scatter(grad_picked)

    small = lax.psum(jnp.stack([grad_route, g_ga1, g_ga2, g_gb1, g_gb2]), ("dp", "seq"))
    small = lax.dynamic_slice_in_dim(
        small, lax.axis_index("dp") * (width // dp_size), width // dp_size, axis=1
    )

    narrow, wide = width // dp_size, OWNERS * width // dp_size

    def columns(own, other, first, count):
        def flat_half(x):
            parts = [x[first + t * narrow : first + (t + 1) * narrow] for t in range(count)]
            return jnp.concatenate(parts, axis=1).astype(F32)

        return both_halves(flat_half(own), flat_half(other), core_first)

    def qkv_columns(own, other):
        parts = [columns(own, other, part * narrow, 1) for part in range(3)]
        return jnp.concatenate(parts, axis=1)

    def down_rows(own, other):
        at = OWNERS * narrow
        return both_halves(
            own[at : at + wide].astype(F32), other[at : at + wide].astype(F32), core_first
        )

    return (
        done_b.astype(BF16),
        grad_input,
        small[0],
        small[1],
        qkv_columns(*mix_a),
        columns(*mix_a, 3 * narrow, 1),
        small[2],
        columns(*feed_a, 0, OWNERS),
        down_rows(*feed_a),
        small[3],
        qkv_columns(*mix_b),
        columns(*mix_b, 3 * narrow, 1),
        small[4],
        columns(*feed_b, 0, OWNERS),
        down_rows(*feed_b),
    )


def solution(mesh):
    tokens, whole, shared = P("dp", "seq", None), P(), P("dp")
    weights = P("dp", None)
    return jax.shard_map(
        per_device,
        mesh=mesh,
        in_specs=(tokens, P("dp", "seq"), P("dp", None)) + (whole,) * 13 + (tokens,),
        out_specs=(tokens, tokens, shared)
        + (shared, weights, weights, shared, weights, weights) * 2,
        check_vma=False,
    )
```

```python
import jax
import jax.numpy as jnp
from jax import lax
from jax.experimental import pallas as pl
from jax.experimental.pallas import tpu as pltpu
from jax.sharding import PartitionSpec as P

HEADS = 12
HEAD_DIM = 64
EPSILON = 1e-06
EXACT = lax.Precision.HIGHEST
F32 = jnp.float32
BF16 = jnp.bfloat16
OWNERS = 4
LANES = 128
BLOCK = 256
VMEM_BYTES = 60 * 1024 * 1024

SMEM_SPEC = pl.BlockSpec(memory_space=pltpu.SMEM)
VMEM_SPEC = pl.BlockSpec(memory_space=pltpu.VMEM)
NT = (((1,), (1,)), ((), ()))
TN = (((0,), (0,)), ((), ()))


def dot(left, right, dims=(((1,), (0,)), ((), ()))):
    return lax.dot_general(left, right, dims, preferred_element_type=F32)


def cost(flops, moved, exps=0):
    return pl.CostEstimate(flops=int(flops), bytes_accessed=int(moved), transcendentals=int(exps))


def project_kernel(tagged, place, x_ref, gain_ref, w_ref, *refs):
    tag_ref, refs = (refs[0], refs[1:]) if tagged else (None, refs)
    act_ref, outs = refs[0], refs[1:]
    rows, width = x_ref.shape[1:]
    half = width // 2
    gain = gain_ref[...].astype(F32).reshape(1, width)
    for i in range(2):
        x = x_ref[i].astype(F32)
        scale = lax.rsqrt(jnp.mean(x * x, axis=-1, keepdims=True) + EPSILON)
        act_ref[i] = (x * scale * gain).astype(BF16)
    for r in (3, 2, 1, 0):
        act = act_ref[place[0] ^ (r >> 1)]
        at = (place[1] ^ (r & 1)) * half
        for part in range(3):
            columns = pl.ds(pl.multiple_of(part * width + at, LANES), half)
            outs[r][part, :rows, :] = dot(act, w_ref[:, columns]).astype(BF16)
            if tagged:
                outs[r][part, rows:, :] = tag_ref[place[0] ^ (r >> 1)]


def project_pieces(place, x, gain, weight, tag=None):
    seqs, rows, width = x.shape
    tagged = tag is not None
    extra = [tag] if tagged else []
    spare = tag.shape[1] if tagged else 0
    piece = jax.ShapeDtypeStruct((3, rows + spare, width // 2), BF16)
    outs = pl.pallas_call(
        lambda *refs: project_kernel(tagged, *refs),
        name="project_pieces",
        out_shape=[jax.ShapeDtypeStruct(x.shape, BF16)] + [piece] * OWNERS,
        in_specs=[SMEM_SPEC] + [VMEM_SPEC] * (3 + len(extra)),
        out_specs=[VMEM_SPEC] * (1 + OWNERS),
        compiler_params=pltpu.CompilerParams(vmem_limit_bytes=VMEM_BYTES),
        cost_estimate=cost(
            2 * seqs * rows * width * 3 * width, 6 * width * width + 12 * seqs * rows * width
        ),
    )(place, x, gain, weight, *extra)
    return outs[0], outs[1:]


def lane_head(head):
    lanes = lax.broadcasted_iota(jnp.int32, (1, LANES), 1)
    return (lanes < HEAD_DIM) if head == 0 else (lanes >= HEAD_DIM)


def only_head(x, head):
    return jnp.where(lane_head(head), x, jnp.zeros_like(x))


def slot_matrix(chosen_ref, counts, r, owner, rows):
    slots = chosen_ref.shape[1]
    spots = chosen_ref[r : r + 1, :]
    row_ids = lax.broadcasted_iota(jnp.int32, (rows, slots), 0)
    slot_ids = lax.broadcasted_iota(jnp.int32, (rows, slots), 1)
    return jnp.where((row_ids == spots) & (slot_ids < counts[owner]), 1.0, 0.0)


def diagonal_mask(counts, query_axis, rows, routed):
    shape = (BLOCK, BLOCK)
    queries = lax.broadcasted_iota(jnp.int32, shape, query_axis)
    keys = lax.broadcasted_iota(jnp.int32, shape, 1 - query_axis)
    if not routed:
        return keys <= queries
    owner = keys // rows
    load = jnp.where(
        owner == 0,
        counts[0],
        jnp.where(owner == 1, counts[1], jnp.where(owner == 2, counts[2], counts[3])),
    )
    live = (keys - owner * rows) < load
    return (keys == queries) | ((keys < queries) & live)


def attend_kernel(rows, routed, place, counts, *refs):
    if routed:
        base, refs = refs[:OWNERS], refs[OWNERS:]
    else:
        chosen_ref, base, slot_in = refs[0], refs[1 : 1 + OWNERS], refs[1 + OWNERS : 1 + 2 * OWNERS]
        refs = refs[1 + 2 * OWNERS :]
    outs, (merged, stats, mixed) = refs[:OWNERS], refs[OWNERS:]
    me = 2 * place[0] + place[1]
    blocks = OWNERS * rows // BLOCK
    for r in range(OWNERS):
        owner = me ^ r
        at = pl.ds(pl.multiple_of(owner * rows, rows), rows)
        if routed:
            for part in range(3):
                merged[part, at, :] = base[r][part]
        else:
            spots = slot_matrix(chosen_ref, counts, r, owner, rows)
            covered = jnp.max(spots, axis=1, keepdims=True) > 0.5
            spots = spots.astype(BF16)
            for part in range(3):
                placed = dot(spots, slot_in[r][part])
                merged[part, at, :] = jnp.where(
                    covered, placed, base[r][part].astype(F32)
                ).astype(BF16)
    visible = diagonal_mask(counts, 0, rows, routed)
    for a in range(blocks):
        queries = merged[0, a * BLOCK : (a + 1) * BLOCK, :] * jnp.asarray(HEAD_DIM**-0.5, BF16)
        mixture = jnp.zeros((BLOCK, LANES), F32)
        stat = jnp.zeros((BLOCK, LANES), F32)
        for head in range(2):
            own = only_head(queries, head)
            scores = []
            for b in range(a + 1):
                keys = merged[1, b * BLOCK : (b + 1) * BLOCK, :]
                found = dot(own, keys, NT)
                scores.append(jnp.where(visible, found, -1e30) if b == a else found)
            top = scores[0]
            for found in scores[1:]:
                top = jnp.maximum(top, found)
            top = jnp.max(top, axis=1, keepdims=True)
            total = jnp.zeros((BLOCK, BLOCK), F32)
            part = jnp.zeros((BLOCK, LANES), F32)
            for b in range(a + 1):
                weight = jnp.exp(scores[b] - top)
                total = total + weight
                values = only_head(merged[2, b * BLOCK : (b + 1) * BLOCK, :], head)
                part = part + dot(weight.astype(BF16), values)
            total = jnp.sum(total, axis=1, keepdims=True)
            mixture = mixture + part * (1.0 / total)
            lane = lax.broadcasted_iota(jnp.int32, (1, LANES), 1)
            stat = jnp.where(lane == head, top + jnp.log(total), stat)
        mixed[a * BLOCK : (a + 1) * BLOCK, :] = mixture.astype(BF16)
        stats[0, :, a * BLOCK : (a + 1) * BLOCK] = stat.T[:8, :]
    for r in range(OWNERS):
        at = pl.ds(pl.multiple_of((me ^ r) * rows, rows), rows)
        outs[r][...] = mixed[at, :]


def attend(place, counts, rows, base, chosen=None, slots=None):
    routed = slots is None
    half = base[0].shape[2]
    pairs = half // LANES
    length = OWNERS * rows
    inputs = [place, counts]
    specs = [SMEM_SPEC, SMEM_SPEC]
    if not routed:
        inputs.append(chosen)
        specs.append(VMEM_SPEC)
    for group, count in ((base, rows), (slots, None if routed else chosen.shape[1])):
        if group is not None:
            inputs += list(group)
            specs += [pl.BlockSpec((3, count, LANES), lambda h: (0, 0, h))] * OWNERS
    blocks = length // BLOCK
    work = blocks * (blocks + 1) // 2 * BLOCK * BLOCK * 2 * pairs
    outs = pl.pallas_call(
        lambda *refs: attend_kernel(rows, routed, *refs),
        name="attend_routed" if routed else "attend_dense",
        grid=(pairs,),
        out_shape=[jax.ShapeDtypeStruct((rows, half), BF16)] * OWNERS
        + [
            jax.ShapeDtypeStruct((3, length, half), BF16),
            jax.ShapeDtypeStruct((pairs, 8, length), F32),
        ],
        in_specs=specs,
        out_specs=[pl.BlockSpec((rows, LANES), lambda h: (0, h))] * OWNERS
        + [
            pl.BlockSpec((3, length, LANES), lambda h: (0, 0, h)),
            pl.BlockSpec((1, 8, length), lambda h: (h, 0, 0)),
        ],
        scratch_shapes=[pltpu.VMEM((length, LANES), BF16)],
        compiler_params=pltpu.CompilerParams(vmem_limit_bytes=VMEM_BYTES),
        cost_estimate=cost(16 * HEAD_DIM * work, 16 * length * half, work),
    )(*inputs)
    return outs[:OWNERS], outs[OWNERS], outs[OWNERS + 1]


def attend_back_kernel(rows, routed, place, counts, *refs):
    if not routed:
        chosen_ref, refs = refs[0], refs[1:]
    merged, stats, grads = refs[0], refs[1], refs[2 : 2 + OWNERS]
    outs, refs = refs[2 + OWNERS : 2 + 2 * OWNERS], refs[2 + 2 * OWNERS :]
    if not routed:
        slot_outs, refs = refs[:OWNERS], refs[OWNERS:]
    incoming, grad_q, grad_k, grad_v = refs
    me = 2 * place[0] + place[1]
    blocks = OWNERS * rows // BLOCK
    for r in range(OWNERS):
        at = pl.ds(pl.multiple_of((me ^ r) * rows, rows), rows)
        incoming[at, :] = grads[r][...]
    for ref in (grad_q, grad_k, grad_v):
        ref[...] = jnp.zeros_like(ref)
    visible = diagonal_mask(counts, 1, rows, routed)
    for a in range(blocks):
        span = slice(a * BLOCK, (a + 1) * BLOCK)
        queries = merged[0, span, :] * jnp.asarray(HEAD_DIM**-0.5, BF16)
        grad_mix = incoming[span, :]
        grad_query = jnp.zeros((BLOCK, LANES), F32)
        for head in range(2):
            own_q = only_head(queries, head)
            own_g = only_head(grad_mix, head)
            level = stats[0, head : head + 1, span]
            probs, grad_probs = [], []
            inner = jnp.zeros((1, BLOCK), F32)
            for b in range(a + 1):
                keys_at = slice(b * BLOCK, (b + 1) * BLOCK)
                prob = jnp.exp(dot(merged[1, keys_at, :], own_q, NT) - level)
                if b == a:
                    prob = jnp.where(visible, prob, 0.0)
                grad_prob = dot(merged[2, keys_at, :], own_g, NT)
                grad_v[keys_at, :] += dot(prob.astype(BF16), own_g)
                inner = inner + jnp.sum(prob * grad_prob, axis=0, keepdims=True)
                probs.append(prob)
                grad_probs.append(grad_prob)
            for b in range(a + 1):
                keys_at = slice(b * BLOCK, (b + 1) * BLOCK)
                grad_score = (probs[b] * (grad_probs[b] - inner)).astype(BF16)
                grad_k[keys_at, :] += dot(grad_score, own_q)
                own_k = only_head(merged[1, keys_at, :], head)
                grad_query = grad_query + dot(grad_score, own_k, TN)
        grad_q[span, :] = grad_query * HEAD_DIM**-0.5
    for r in range(OWNERS):
        owner = me ^ r
        at = pl.ds(pl.multiple_of(owner * rows, rows), rows)
        if not routed:
            spots = slot_matrix(chosen_ref, counts, r, owner, rows).astype(BF16)
        for part, ref in enumerate((grad_q, grad_k, grad_v)):
            found = ref[at, :].astype(BF16)
            outs[r][part] = found
            if not routed:
                slot_outs[r][part] = dot(spots, found, TN).astype(BF16)


def attend_back(place, counts, merged, stats, grads, chosen=None):
    routed = chosen is None
    rows, half = grads[0].shape
    pairs = half // LANES
    length = OWNERS * rows
    inputs = [place, counts]
    specs = [SMEM_SPEC, SMEM_SPEC]
    shapes = [jax.ShapeDtypeStruct((3, rows, half), BF16)] * OWNERS
    out_specs = [pl.BlockSpec((3, rows, LANES), lambda h: (0, 0, h))] * OWNERS
    if not routed:
        inputs.append(chosen)
        specs.append(VMEM_SPEC)
        slots = chosen.shape[1]
        shapes += [jax.ShapeDtypeStruct((3, slots, half), BF16)] * OWNERS
        out_specs += [pl.BlockSpec((3, slots, LANES), lambda h: (0, 0, h))] * OWNERS
    inputs += [merged, stats] + list(grads)
    specs += [
        pl.BlockSpec((3, length, LANES), lambda h: (0, 0, h)),
        pl.BlockSpec((1, 8, length), lambda h: (h, 0, 0)),
    ] + [pl.BlockSpec((rows, LANES), lambda h: (0, h))] * OWNERS
    blocks = length // BLOCK
    work = blocks * (blocks + 1) // 2 * BLOCK * BLOCK * 2 * pairs
    outs = pl.pallas_call(
        lambda *refs: attend_back_kernel(rows, routed, *refs),
        name="attend_routed_back" if routed else "attend_dense_back",
        grid=(pairs,),
        out_shape=shapes,
        in_specs=specs,
        out_specs=out_specs,
        scratch_shapes=[pltpu.VMEM((length, LANES), BF16)]
        + [pltpu.VMEM((length, LANES), F32)] * 3,
        compiler_params=pltpu.CompilerParams(vmem_limit_bytes=VMEM_BYTES),
        cost_estimate=cost(40 * HEAD_DIM * work, 16 * length * half, work),
    )(*inputs)
    return outs[:OWNERS], outs[OWNERS:]


SPARE = 32
Y_STAGE = -1


def send_orders(bits):
    dp = list(range(bits))
    rest = dp[2:]
    return (
        [dp[0], Y_STAGE, dp[1]] + rest,
        [dp[1], dp[0], Y_STAGE] + rest,
        [Y_STAGE, dp[0], dp[1]] + rest,
    )


def position(order, slab, y_half):
    spot = 0
    for k in order:
        spot = 2 * spot + (y_half if k == Y_STAGE else ((slab >> k) & 1))
    return spot


def store_slabs(target, bits, place, first, found, rows):
    ref, at, which = target
    order = send_orders(bits)[which]
    part = rows // 2
    for d in range(found.shape[0] // rows):
        for y_half in range(2):
            spot = position(order, first + d, y_half) ^ place[2 + which]
            low = d * rows + y_half * part
            ref[pl.ds(spot, 1), at // 2 : at // 2 + part, :] = found[low : low + part].astype(
                BF16
            )[None]


def feed_grad_kernel(bits, orders, routed, place, *refs):
    ff_refs, gel_refs, mix_refs, gh_refs, gff_refs, gatt_refs = (
        refs[2 * k : 2 * k + 2] for k in range(6)
    )
    refs = refs[12:]
    width = ff_refs[0].shape[1]
    half = width // 2
    slabs = 1 << bits
    narrow = width // slabs
    wide = OWNERS * narrow
    first, second = refs[-2:]
    if routed:
        for d in range(slabs):
            store_slabs((first, wide, orders[0]), bits, place, d, refs[0][d], SPARE)
    own = pl.ds(pl.multiple_of(place[1] * half, LANES), half)
    turned = [ref[...].T for ref in ff_refs]
    for t in range(OWNERS):
        tile = pl.ds(pl.multiple_of((place[1] * OWNERS + t) * half, LANES), half)
        found = dot(turned[0], gh_refs[0][:, tile])
        found = found + dot(turned[1], gh_refs[1][:, t * half : (t + 1) * half])
        store_slabs((first, t * narrow, orders[0]), bits, place, 0, found, narrow)
    for t in range(OWNERS):
        rows = slice(t * width, (t + 1) * width)
        found = dot(gel_refs[0][:, rows], gff_refs[0][:, own], TN)
        found = found + dot(gel_refs[1][:, rows], gff_refs[1][...], TN)
        store_slabs((second, 0, orders[1]), bits, place, t * slabs // OWNERS, found, wide)
    found = dot(mix_refs[0][...], gatt_refs[0][:, own], TN)
    found = found + dot(mix_refs[1][...], gatt_refs[1][...], TN)
    store_slabs((second, wide, orders[1]), bits, place, 0, found, narrow)


def feed_grad(place, bits, orders, operands, route=None):
    tokens, width = operands[0].shape
    half = width // 2
    slabs = 1 << bits
    narrow = width // slabs
    wide = OWNERS * narrow
    routed = route is not None
    rows = (wide + (SPARE if routed else 0), wide + narrow)
    extra = [route] if routed else []
    return pl.pallas_call(
        lambda *refs: feed_grad_kernel(bits, orders, routed, *refs),
        name="feed_grad",
        in_specs=[SMEM_SPEC] + [VMEM_SPEC] * (12 + len(extra)),
        out_specs=[VMEM_SPEC] * len(rows),
        out_shape=[jax.ShapeDtypeStruct((2 * slabs, count // 2, half), BF16) for count in rows],
        compiler_params=pltpu.CompilerParams(vmem_limit_bytes=VMEM_BYTES),
        cost_estimate=cost(
            18 * tokens * width * width, 9 * width * width + 40 * tokens * width
        ),
    )(place, *operands, *extra)


def qkv_grad_kernel(bits, order, place, *refs):
    acts, pieces, out = refs[:OWNERS], refs[OWNERS : 2 * OWNERS], refs[2 * OWNERS]
    narrow = acts[0].shape[1] // (1 << bits)
    for part in range(3):
        found = dot(acts[0][...], pieces[0][part], TN)
        for r in range(1, OWNERS):
            found = found + dot(acts[r][...], pieces[r][part], TN)
        store_slabs((out, part * narrow, order), bits, place, 0, found, narrow)


def qkv_grad(place, bits, order, acts, pieces):
    rows, width = acts[0].shape
    half = width // 2
    slabs = 1 << bits
    narrow = width // slabs
    return pl.pallas_call(
        lambda *refs: qkv_grad_kernel(bits, order, *refs),
        name="qkv_grad",
        in_specs=[SMEM_SPEC] + [VMEM_SPEC] * (2 * OWNERS),
        out_specs=VMEM_SPEC,
        out_shape=jax.ShapeDtypeStruct((2 * slabs, 3 * narrow // 2, half), BF16),
        compiler_params=pltpu.CompilerParams(vmem_limit_bytes=VMEM_BYTES),
        cost_estimate=cost(
            12 * rows * width * width, 3 * width * width + 20 * rows * width
        ),
    )(place, *acts, *pieces)


def finish_kernel(down_at, place, near_ref, far_ref, qkv_ref, out_ref, up_ref, down_ref):
    narrow, width = out_ref.shape
    half = width // 2
    wide = OWNERS * narrow

    for flip, ref in ((0, near_ref), (1, far_ref)):
        side = place[1] ^ flip

        def put(out, tile, at, rows):
            columns = pl.ds(pl.multiple_of(tile * half, LANES), half)
            for y_half in range(2):
                part = rows // 2
                out[y_half * part : (y_half + 1) * part, columns] = ref[
                    y_half, at // 2 : at // 2 + part, :
                ].astype(F32)

        for t in range(OWNERS):
            put(up_ref, side * OWNERS + t, t * narrow, narrow)
        put(down_ref, side, down_at, wide)
        put(out_ref, side, down_at + wide, narrow)
        for p in range(3):
            put(qkv_ref, 2 * p + side, down_at + wide + (1 + p) * narrow, narrow)


def finish(place, down_at, narrow, width, near, far):
    shapes = [(narrow, 3 * width), (narrow, width), (narrow, 4 * width), (4 * narrow, width)]
    return pl.pallas_call(
        lambda *refs: finish_kernel(down_at, *refs),
        name="finish_grads",
        in_specs=[SMEM_SPEC] + [VMEM_SPEC] * 2,
        out_specs=[VMEM_SPEC] * 4,
        out_shape=[jax.ShapeDtypeStruct(shape, F32) for shape in shapes],
        compiler_params=pltpu.CompilerParams(vmem_limit_bytes=VMEM_BYTES),
        cost_estimate=cost(0, 72 * narrow * width),
    )(place, near, far)


def swap(x, axis, bit):
    size = lax.axis_size(axis)
    return lax.ppermute(x, axis, [(i, i ^ bit) for i in range(size)])


def exchange(pieces):
    return [pieces[0]] + [swap(pieces[r], "seq", r) for r in range(1, OWNERS)]


def add_low(a, b):
    return (a.astype(F32) + b.astype(F32)).astype(BF16)


def halves(unit):
    n = unit.shape[0] // 2
    return unit[:n], unit[n:]


def combine(keep, received):
    if keep.shape[0] == 1:
        return add_low(keep, received)[0]
    (low, high), (low_in, high_in) = halves(keep), halves(received)
    return add_low(low, low_in), add_low(high, high_in)


def stage_swap(state, order, stage):
    k = order[stage]
    return swap(state[1], "seq", 2) if k == Y_STAGE else swap(state[1], "dp", 1 << k)


class Chain:
    def __init__(self, unit, order):
        self.state, self.order, self.stage = halves(unit), order, 0

    def step(self, after):
        keep, _ = hold(self.state[0], after)
        self.state = combine(keep, stage_swap(self.state, self.order, self.stage))
        self.stage += 1
        return self.state


def gather_halves(own, y_first):
    other = swap(own, "seq", 2)
    pair = jnp.stack([jnp.where(y_first, own, other), jnp.where(y_first, other, own)])
    return pair, swap(pair, "seq", 1)


def hold(*values):
    return lax.optimization_barrier(values)


def both_halves(own, other, first):
    return jnp.concatenate(
        [jnp.where(first, own, other), jnp.where(first, other, own)], axis=-1
    )


def assemble(pieces, y_first, core_first):
    near = both_halves(pieces[0], pieces[1], core_first)
    far = both_halves(pieces[2], pieces[3], core_first)
    return jnp.stack([jnp.where(y_first, near, far), jnp.where(y_first, far, near)])


def assemble_packed(pieces, y_first, core_first):
    found = assemble(pieces, y_first, core_first)
    return jnp.concatenate([found[:, 0], found[:, 1], found[:, 2]], axis=-1)


def core_half(x, at):
    half = x.shape[-1] // 2
    return lax.dynamic_slice_in_dim(x, at * half, half, axis=x.ndim - 1)


def with_far(x):
    return x, swap(x, "seq", 1)


def half_with_far(x, core_at):
    return x, swap(core_half(x, 1 - core_at), "seq", 1)


def split_pieces(x, place):
    half = x.shape[-1] // 2
    found = []
    for r in range(OWNERS):
        rows = lax.dynamic_index_in_dim(x, place[0] ^ (r >> 1), 0, keepdims=False)
        found.append(lax.dynamic_slice_in_dim(rows, (place[1] ^ (r & 1)) * half, half, axis=1))
    return found


def norm_rows(vector, gain_vec):
    return (
        vector * lax.rsqrt(jnp.mean(vector * vector, axis=-1, keepdims=True) + EPSILON) * gain_vec
    )


def project(left_side, weight):
    return jnp.einsum("bnd,de->bne", left_side, weight, preferred_element_type=F32)


def project_back(gradient, weight):
    return jnp.einsum("bne,de->bnd", gradient, weight, preferred_element_type=F32)


def feed_forward(resid, router, mixture, w_out, gain_two, w_up, w_down):
    attended = project(mixture, w_out)
    middle = resid + attended if router is None else resid + router[..., None] * attended
    ff_in = norm_rows(middle, gain_two.astype(F32)).astype(BF16)
    hidden = project(ff_in, w_up)
    activated = jax.nn.gelu(hidden).astype(BF16)
    done = middle + project(activated, w_down)
    return done, (attended, middle, ff_in, hidden, activated)


def feed_backward(grad_done, router, w_out, gain_two, w_up, w_down, kept):
    attended, middle, ff_in, hidden, activated = kept
    grad_ff = grad_done.astype(BF16)
    grad_act = project_back(grad_ff, w_down)
    unused_value, gelu_pull = jax.vjp(jax.nn.gelu, hidden)
    grad_hidden = gelu_pull(grad_act)[0].astype(BF16)
    grad_ffin = project_back(grad_hidden, w_up)
    grad_middle = grad_done + norm_back(middle, gain_two, grad_ffin)
    scaled = grad_middle if router is None else router[..., None] * grad_middle
    grad_attended = scaled.astype(BF16)
    grad_mixture = project_back(grad_attended, w_out).astype(BF16)
    return grad_ff, grad_hidden, grad_middle, grad_attended, grad_mixture


def norm_back(x, gain, grad_act_in):
    unused, pull = jax.vjp(lambda x: norm_rows(x, gain.astype(F32)), x)
    return pull(grad_act_in)[0]


def per_device(
    stream_in,
    chosen,
    counts,
    route_w,
    gain_a1,
    qkv_a,
    out_a,
    gain_a2,
    up_a,
    down_a,
    gain_b1,
    qkv_b,
    out_b,
    gain_b2,
    up_b,
    down_b,
    cotangent,
):
    seqs, rows, width = stream_in.shape
    slots = chosen.shape[1]
    half = width // 2
    dp_size = lax.axis_size("dp")
    bits = dp_size.bit_length() - 1
    narrow = width // dp_size
    me = lax.axis_index("seq")
    dp_at = lax.axis_index("dp")
    y_at, core_at = me // 2, me % 2
    y_first, core_first = y_at == 0, core_at == 0
    orders = send_orders(bits)
    place = jnp.stack(
        [y_at, core_at] + [position(order, dp_at, y_at) for order in orders]
    ).astype(jnp.int32)
    counts_mine = lax.dynamic_index_in_dim(counts, y_at, 0, keepdims=False)
    own_load = lax.dynamic_index_in_dim(counts, me, 1, keepdims=False)
    live = jnp.arange(slots, dtype=jnp.int32)[None, :] < own_load[:, None]
    hits = chosen[:, :, None] == jnp.arange(rows, dtype=jnp.int32)
    gather = hits.astype(BF16)
    live_hits = (hits & live[..., None]).astype(F32)
    covered = jnp.any(hits & live[..., None], axis=1)[..., None]
    tag = jnp.pad(chosen.astype(BF16), ((0, 0), (0, LANES - slots)))
    tag = jnp.pad(jnp.tile(tag, (1, half // LANES))[:, None, :], ((0, 0), (0, 15), (0, 0)))

    def scatter(values):
        return jnp.einsum("bcr,bcd->brd", live_hits, values, precision=EXACT)

    def flat(x):
        return x.reshape(x.shape[0] * x.shape[1], x.shape[2])

    picked = jnp.einsum("bcr,brd->bcd", gather, stream_in, preferred_element_type=F32)
    picked_low = picked.astype(BF16)
    router = jnp.einsum("bcd,d->bc", picked_low, route_w, preferred_element_type=F32)
    act_a, pieces = project_pieces(place, picked_low, gain_a1, qkv_a)
    pieces = exchange(pieces)
    act_base, base = project_pieces(place, stream_in, gain_b1, qkv_b, tag)
    base_two = swap(base[2], "seq", 2)
    mixed, merged_a, stats_a = attend(place, counts_mine, slots, pieces)
    mixed = exchange(mixed)
    mixed, late = hold(mixed, (base[1], base[3]))
    base = [base[0], swap(late[0], "seq", 1), base_two, swap(late[1], "seq", 3)]
    mixture_a = assemble(mixed, y_first, core_first)
    done_a, kept_a = feed_forward(picked, router, mixture_a, out_a, gain_a2, up_a, down_a)
    change = jnp.where(live[..., None], done_a - picked, 0.0)
    slot_mid = picked + change
    base_three, slot_mid = hold(base[3], slot_mid)
    base = base[:3] + [base_three]
    act_slot, slot_pieces = project_pieces(place, slot_mid, gain_b1, qkv_b)
    slot_pieces = exchange(slot_pieces)
    chosen_mine = jnp.concatenate(
        [piece[0, rows : rows + 1, :slots] for piece in base], axis=0
    ).astype(jnp.int32)
    act_b = jnp.where(
        covered,
        jnp.einsum("bcr,bcd->brd", live_hits.astype(BF16), act_slot, preferred_element_type=F32),
        act_base.astype(F32),
    ).astype(BF16)
    acts = jnp.concatenate([act_b, act_a], axis=1)
    acts_near = lax.dynamic_index_in_dim(acts, y_at, 0, keepdims=False)
    acts_far = lax.dynamic_index_in_dim(acts, 1 - y_at, 0, keepdims=False)
    middle = stream_in.astype(F32) + scatter(change)
    slot_pieces, acts_near, acts_far, middle = hold(slot_pieces, acts_near, acts_far, middle)
    acts_pair = jnp.stack([acts_near, swap(acts_far, "seq", 2)])
    mixed, merged_b, stats_b = attend(
        place, counts_mine, rows, base, chosen_mine, slot_pieces
    )
    acts_other = swap(acts_pair, "seq", 1)
    acts = [acts_pair[0], acts_other[0], acts_pair[1], acts_other[1]]
    acts_b = [x[:rows] for x in acts]
    acts_a = [x[rows:] for x in acts]
    mixture_b = assemble(exchange(mixed), y_first, core_first)
    done_b, kept_b = feed_forward(middle, None, mixture_b, out_b, gain_b2, up_b, down_b)

    x_first, z_first, y_first_order = orders
    flat_b = [flat(x) for x in (kept_b[2], kept_b[4], mixture_b)]
    early = [with_far(x) for x in flat_b]
    early_grad = half_with_far(flat(cotangent), core_at)
    grad_ff_b, grad_hidden_b, grad_mid_b, grad_att_b, grad_mix_b = feed_backward(
        cotangent.astype(F32), None, out_b, gain_b2, up_b, down_b, kept_b
    )
    grads = split_pieces(grad_mix_b, place)
    late = [half_with_far(flat(x), core_at) for x in (grad_hidden_b, grad_att_b)]
    grads, early = hold(grads, early)
    grads = exchange(grads)
    operands = [y for x in early + [late[0], early_grad, late[1]] for y in x]
    feed_b = feed_grad(place, bits, (0, 1), operands)
    grads, feed_b = hold(grads, feed_b)
    up_chain, down_chain = Chain(feed_b[0], x_first), Chain(feed_b[1], z_first)
    packed_b, packed_slot = attend_back(place, counts_mine, merged_b, stats_b, grads, chosen_mine)
    packed_slot = exchange(packed_slot)
    part_b = qkv_grad(place, bits, 0, acts_b, packed_b)
    token = up_chain.step(part_b)
    token = down_chain.step(token)
    packed_slot, part_b, packed_b, token = hold(packed_slot, part_b, packed_b, token)
    part_chain = Chain(part_b, x_first)
    packed_b_two = swap(packed_b[2], "seq", 2)

    grad_packed_slot = assemble_packed(packed_slot, y_first, core_first)
    slot_grad = norm_back(slot_mid, gain_b1, project_back(grad_packed_slot, qkv_b))
    mid_at_slot = jnp.einsum("bcr,brd->bcd", live_hits, grad_mid_b, precision=EXACT)
    grad_done = jnp.where(live[..., None], mid_at_slot + slot_grad, 0.0)
    early = [with_far(flat(x)) for x in (kept_a[2], kept_a[4], mixture_a)]
    grad_ff_a, grad_hidden_a, grad_mid_a, grad_att_a, grad_mix_a = feed_backward(
        grad_done, router, out_a, gain_a2, up_a, down_a, kept_a
    )
    grads = split_pieces(grad_mix_a, place)
    late = [
        half_with_far(flat(x), core_at) for x in (grad_hidden_a, grad_ff_a, grad_att_a)
    ]
    grads, early = hold(grads, early)
    grads = exchange(grads)
    grad_router = jnp.sum(kept_a[0] * grad_mid_a, axis=-1)
    grad_route = jnp.einsum("bc,bcd->d", grad_router, picked, precision=EXACT)
    route = jnp.pad(
        grad_route.reshape(dp_size, 1, narrow), ((0, 0), (0, SPARE - 1), (0, half - narrow))
    )
    operands = [y for x in early + late for y in x]
    feed_a = feed_grad(place, bits, (0, 1), operands, route)
    token = up_chain.step(feed_a)
    token = down_chain.step(token)
    grads, feed_a, token = hold(grads, feed_a, token)
    up_chain_a, down_chain_a = Chain(feed_a[0], x_first), Chain(feed_a[1], z_first)
    packed_a, _ = attend_back(place, counts_mine, merged_a, stats_a, grads)
    returned_a = exchange(packed_a)
    part_a = qkv_grad(place, bits, 2, acts_a, packed_a)
    token = part_chain.step(part_a)
    token = up_chain.step(token)
    token = down_chain.step(token)
    returned_a, part_a, token = hold(returned_a, part_a, token)
    part_chain_a = Chain(part_a, y_first_order)

    grad_packed_a = assemble_packed(returned_a, y_first, core_first)
    res_a = norm_back(picked, gain_a1, project_back(grad_packed_a, qkv_a))
    grad_picked = (
        grad_mid_a + res_a + grad_router[..., None] * route_w.astype(F32) - grad_done
    )
    token = up_chain_a.step((token, grad_picked))
    token = down_chain_a.step(token)
    token = part_chain.step(token)
    token = up_chain.step(token)
    token = down_chain.step(token)
    token = part_chain_a.step(token)
    token = part_chain.step(token)
    for chain in (up_chain, down_chain):
        while chain.stage < len(chain.order):
            token = chain.step(token)
    token = up_chain_a.step(token)
    while part_chain.stage < len(part_chain.order):
        token = part_chain.step(token)
    late, token = hold((packed_b[1], packed_b[3]), token)
    returned_b = [packed_b[0], swap(late[0], "seq", 1), packed_b_two, swap(late[1], "seq", 3)]
    token = down_chain_a.step(token)
    token = part_chain_a.step(token)
    near_b, far_b = gather_halves(
        jnp.concatenate([up_chain.state, down_chain.state, part_chain.state]), y_first
    )
    token = up_chain_a.step(token)
    token = down_chain_a.step(token)
    token = part_chain_a.step(token)
    for chain in (up_chain_a, down_chain_a, part_chain_a):
        while chain.stage < len(chain.order) - 1:
            token = chain.step(token)

    grad_packed_b = assemble_packed(returned_b, y_first, core_first)
    res_b = norm_back(middle, gain_b1, project_back(grad_packed_b, qkv_b))
    grad_input = grad_mid_b + res_b + scatter(grad_picked)
    qkv_gb, out_gb, up_gb, down_gb = finish(place, OWNERS * narrow, narrow, width, near_b, far_b)
    token = (token, qkv_gb, grad_input)
    for chain in (up_chain_a, down_chain_a, part_chain_a):
        token = chain.step(token)
    near, far = gather_halves(
        jnp.concatenate([up_chain_a.state, down_chain_a.state, part_chain_a.state]), y_first
    )
    down_at = OWNERS * narrow + SPARE
    qkv_ga, out_ga, up_ga, down_ga = finish(place, down_at, narrow, width, near, far)
    at = OWNERS * narrow // 2
    route = near[0, at, :narrow].astype(F32) + far[0, at, :narrow].astype(F32)

    def gain_grad(found, weight, gain):
        at = dp_at * narrow
        weight = lax.dynamic_slice_in_dim(weight, at, narrow, axis=0).astype(F32)
        gain = lax.dynamic_slice_in_dim(gain, at, narrow, axis=0).astype(F32)
        return jnp.sum(found * weight, axis=1) / gain

    return (
        done_b.astype(BF16),
        grad_input,
        route,
        gain_grad(qkv_ga, qkv_a, gain_a1),
        qkv_ga,
        out_ga,
        gain_grad(up_ga, up_a, gain_a2),
        up_ga,
        down_ga,
        gain_grad(qkv_gb, qkv_b, gain_b1),
        qkv_gb,
        out_gb,
        gain_grad(up_gb, up_b, gain_b2),
        up_gb,
        down_gb,
    )


def solution(mesh):
    tokens, whole, shared = P("dp", "seq", None), P(), P("dp")
    weights = P("dp", None)
    return jax.shard_map(
        per_device,
        mesh=mesh,
        in_specs=(tokens, P("dp", "seq"), P("dp", None)) + (whole,) * 13 + (tokens,),
        out_specs=(tokens, tokens, shared)
        + (shared, weights, weights, shared, weights, weights) * 2,
        check_vma=False,
    )
```

```python
import jax
import jax.numpy as jnp
from jax import lax
from jax.experimental import pallas as pl
from jax.experimental.pallas import tpu as pltpu
from jax.sharding import PartitionSpec as P

HEADS = 12
HEAD_DIM = 64
EPSILON = 1e-06
EXACT = lax.Precision.HIGHEST
F32 = jnp.float32
BF16 = jnp.bfloat16
OWNERS = 4
LANES = 128
BLOCK = 256
VMEM_BYTES = 60 * 1024 * 1024

SMEM_SPEC = pl.BlockSpec(memory_space=pltpu.SMEM)
VMEM_SPEC = pl.BlockSpec(memory_space=pltpu.VMEM)
NT = (((1,), (1,)), ((), ()))
TN = (((0,), (0,)), ((), ()))


def dot(left, right, dims=(((1,), (0,)), ((), ()))):
    return lax.dot_general(left, right, dims, preferred_element_type=F32)


def cost(flops, moved, exps=0):
    return pl.CostEstimate(flops=int(flops), bytes_accessed=int(moved), transcendentals=int(exps))


def project_kernel(tagged, place, x_ref, gain_ref, w_ref, *refs):
    tag_ref, refs = (refs[0], refs[1:]) if tagged else (None, refs)
    act_ref, outs = refs[0], refs[1:]
    rows, width = x_ref.shape[1:]
    half = width // 2
    gain = gain_ref[...].astype(F32).reshape(1, width)
    for i in range(2):
        x = x_ref[i].astype(F32)
        scale = lax.rsqrt(jnp.mean(x * x, axis=-1, keepdims=True) + EPSILON)
        act_ref[i] = (x * scale * gain).astype(BF16)
    for r in (3, 2, 1, 0):
        act = act_ref[place[0] ^ (r >> 1)]
        at = (place[1] ^ (r & 1)) * half
        for part in range(3):
            columns = pl.ds(pl.multiple_of(part * width + at, LANES), half)
            outs[r][part, :rows, :] = dot(act, w_ref[:, columns]).astype(BF16)
            if tagged:
                outs[r][part, rows:, :] = tag_ref[place[0] ^ (r >> 1)]


def project_pieces(place, x, gain, weight, tag=None):
    seqs, rows, width = x.shape
    tagged = tag is not None
    extra = [tag] if tagged else []
    spare = tag.shape[1] if tagged else 0
    piece = jax.ShapeDtypeStruct((3, rows + spare, width // 2), BF16)
    outs = pl.pallas_call(
        lambda *refs: project_kernel(tagged, *refs),
        name="project_pieces",
        out_shape=[jax.ShapeDtypeStruct(x.shape, BF16)] + [piece] * OWNERS,
        in_specs=[SMEM_SPEC] + [VMEM_SPEC] * (3 + len(extra)),
        out_specs=[VMEM_SPEC] * (1 + OWNERS),
        compiler_params=pltpu.CompilerParams(vmem_limit_bytes=VMEM_BYTES),
        cost_estimate=cost(
            2 * seqs * rows * width * 3 * width, 6 * width * width + 12 * seqs * rows * width
        ),
    )(place, x, gain, weight, *extra)
    return outs[0], outs[1:]


def lane_head(head):
    lanes = lax.broadcasted_iota(jnp.int32, (1, LANES), 1)
    return (lanes < HEAD_DIM) if head == 0 else (lanes >= HEAD_DIM)


def only_head(x, head):
    return jnp.where(lane_head(head), x, jnp.zeros_like(x))


def slot_matrix(chosen_ref, counts, r, owner, rows):
    slots = chosen_ref.shape[1]
    spots = chosen_ref[r : r + 1, :]
    row_ids = lax.broadcasted_iota(jnp.int32, (rows, slots), 0)
    slot_ids = lax.broadcasted_iota(jnp.int32, (rows, slots), 1)
    return jnp.where((row_ids == spots) & (slot_ids < counts[owner]), 1.0, 0.0)


def diagonal_mask(counts, query_axis, rows, routed):
    shape = (BLOCK, BLOCK)
    queries = lax.broadcasted_iota(jnp.int32, shape, query_axis)
    keys = lax.broadcasted_iota(jnp.int32, shape, 1 - query_axis)
    if not routed:
        return keys <= queries
    owner = keys // rows
    load = jnp.where(
        owner == 0,
        counts[0],
        jnp.where(owner == 1, counts[1], jnp.where(owner == 2, counts[2], counts[3])),
    )
    live = (keys - owner * rows) < load
    return (keys == queries) | ((keys < queries) & live)


def attend_kernel(rows, routed, place, counts, *refs):
    if routed:
        base, refs = refs[:OWNERS], refs[OWNERS:]
    else:
        chosen_ref, base, slot_in = refs[0], refs[1 : 1 + OWNERS], refs[1 + OWNERS : 1 + 2 * OWNERS]
        refs = refs[1 + 2 * OWNERS :]
    outs, (merged, mixed, stats) = refs[:OWNERS], refs[OWNERS:]
    me = 2 * place[0] + place[1]
    blocks = OWNERS * rows // BLOCK
    for r in range(OWNERS):
        owner = me ^ r
        at = pl.ds(pl.multiple_of(owner * rows, rows), rows)
        if routed:
            for part in range(3):
                merged[part, at, :] = base[r][part]
        else:
            spots = slot_matrix(chosen_ref, counts, r, owner, rows)
            covered = jnp.max(spots, axis=1, keepdims=True) > 0.5
            spots = spots.astype(BF16)
            for part in range(3):
                placed = dot(spots, slot_in[r][part])
                merged[part, at, :] = jnp.where(
                    covered, placed, base[r][part].astype(F32)
                ).astype(BF16)
    visible = diagonal_mask(counts, 0, rows, routed)
    for a in range(blocks):
        queries = merged[0, a * BLOCK : (a + 1) * BLOCK, :] * jnp.asarray(HEAD_DIM**-0.5, BF16)
        mixture = jnp.zeros((BLOCK, LANES), F32)
        stat = jnp.zeros((BLOCK, LANES), F32)
        for head in range(2):
            own = only_head(queries, head)
            scores = []
            for b in range(a + 1):
                keys = merged[1, b * BLOCK : (b + 1) * BLOCK, :]
                found = dot(own, keys, NT)
                scores.append(jnp.where(visible, found, -1e30) if b == a else found)
            top = scores[0]
            for found in scores[1:]:
                top = jnp.maximum(top, found)
            top = jnp.max(top, axis=1, keepdims=True)
            part = jnp.zeros((BLOCK, LANES), F32)
            for b in range(a + 1):
                weight = jnp.exp(scores[b] - top).astype(BF16)
                values = merged[2, b * BLOCK : (b + 1) * BLOCK, :]
                part = part + dot(weight, jnp.where(lane_head(head), values, jnp.ones_like(values)))
            turned = pltpu.roll(part, HEAD_DIM, axis=1)
            mixture = jnp.where(lane_head(head), part * (1.0 / turned), mixture)
            total = turned if head == 0 else part
            lane = lax.broadcasted_iota(jnp.int32, (1, LANES), 1)
            stat = jnp.where(lane == head, top + jnp.log(total), stat)
        mixed[a * BLOCK : (a + 1) * BLOCK, :] = mixture.astype(BF16)
        stats[0, :, a * BLOCK : (a + 1) * BLOCK] = stat.T[:8, :]
    for r in range(OWNERS):
        at = pl.ds(pl.multiple_of((me ^ r) * rows, rows), rows)
        outs[r][...] = mixed[at, :]


def attend(place, counts, rows, base, chosen=None, slots=None):
    routed = slots is None
    half = base[0].shape[2]
    pairs = half // LANES
    length = OWNERS * rows
    inputs = [place, counts]
    specs = [SMEM_SPEC, SMEM_SPEC]
    if not routed:
        inputs.append(chosen)
        specs.append(VMEM_SPEC)
    for group, count in ((base, rows), (slots, None if routed else chosen.shape[1])):
        if group is not None:
            inputs += list(group)
            specs += [pl.BlockSpec((3, count, LANES), lambda h: (0, 0, h))] * OWNERS
    blocks = length // BLOCK
    work = blocks * (blocks + 1) // 2 * BLOCK * BLOCK * 2 * pairs
    outs = pl.pallas_call(
        lambda *refs: attend_kernel(rows, routed, *refs),
        name="attend_routed" if routed else "attend_dense",
        grid=(pairs,),
        out_shape=[jax.ShapeDtypeStruct((rows, half), BF16)] * OWNERS
        + [
            jax.ShapeDtypeStruct((3, length, half), BF16),
            jax.ShapeDtypeStruct((length, half), BF16),
            jax.ShapeDtypeStruct((pairs, 8, length), F32),
        ],
        in_specs=specs,
        out_specs=[pl.BlockSpec((rows, LANES), lambda h: (0, h))] * OWNERS
        + [
            pl.BlockSpec((3, length, LANES), lambda h: (0, 0, h)),
            pl.BlockSpec((length, LANES), lambda h: (0, h)),
            pl.BlockSpec((1, 8, length), lambda h: (h, 0, 0)),
        ],
        compiler_params=pltpu.CompilerParams(vmem_limit_bytes=VMEM_BYTES),
        cost_estimate=cost(16 * HEAD_DIM * work, 16 * length * half, work),
    )(*inputs)
    return outs[:OWNERS], outs[OWNERS:]


def attend_back_kernel(rows, routed, place, counts, *refs):
    if not routed:
        chosen_ref, refs = refs[0], refs[1:]
    merged, mixed, stats, grads = refs[0], refs[1], refs[2], refs[3 : 3 + OWNERS]
    outs, refs = refs[3 + OWNERS : 3 + 2 * OWNERS], refs[3 + 2 * OWNERS :]
    if not routed:
        slot_outs, refs = refs[:OWNERS], refs[OWNERS:]
    incoming, grad_q, grad_k, grad_v = refs
    me = 2 * place[0] + place[1]
    blocks = OWNERS * rows // BLOCK
    for r in range(OWNERS):
        at = pl.ds(pl.multiple_of((me ^ r) * rows, rows), rows)
        incoming[at, :] = grads[r][...]
    for ref in (grad_q, grad_k, grad_v):
        ref[...] = jnp.zeros_like(ref)
    visible = diagonal_mask(counts, 1, rows, routed)
    for a in range(blocks):
        span = slice(a * BLOCK, (a + 1) * BLOCK)
        queries = merged[0, span, :] * jnp.asarray(HEAD_DIM**-0.5, BF16)
        grad_mix = incoming[span, :]
        grad_query = jnp.zeros((BLOCK, LANES), F32)
        inner = (grad_mix.astype(F32) * mixed[span, :].astype(F32)).T
        for head in range(2):
            own_q = only_head(queries, head)
            own_g = only_head(grad_mix, head)
            level = stats[0, head : head + 1, span]
            offset = jnp.sum(
                inner[head * HEAD_DIM : (head + 1) * HEAD_DIM], axis=0, keepdims=True
            )
            for b in range(a + 1):
                keys_at = slice(b * BLOCK, (b + 1) * BLOCK)
                prob = jnp.exp(dot(merged[1, keys_at, :], own_q, NT) - level)
                if b == a:
                    prob = jnp.where(visible, prob, 0.0)
                grad_prob = dot(merged[2, keys_at, :], own_g, NT)
                grad_v[keys_at, :] += dot(prob.astype(BF16), own_g)
                grad_score = (prob * (grad_prob - offset)).astype(BF16)
                grad_k[keys_at, :] += dot(grad_score, own_q)
                own_k = only_head(merged[1, keys_at, :], head)
                grad_query = grad_query + dot(grad_score, own_k, TN)
        grad_q[span, :] = grad_query * HEAD_DIM**-0.5
    for r in range(OWNERS):
        owner = me ^ r
        at = pl.ds(pl.multiple_of(owner * rows, rows), rows)
        if not routed:
            spots = slot_matrix(chosen_ref, counts, r, owner, rows).astype(BF16)
        for part, ref in enumerate((grad_q, grad_k, grad_v)):
            found = ref[at, :].astype(BF16)
            outs[r][part] = found
            if not routed:
                slot_outs[r][part] = dot(spots, found, TN).astype(BF16)


def attend_back(place, counts, saved, grads, chosen=None):
    routed = chosen is None
    rows, half = grads[0].shape
    pairs = half // LANES
    length = OWNERS * rows
    inputs = [place, counts]
    specs = [SMEM_SPEC, SMEM_SPEC]
    shapes = [jax.ShapeDtypeStruct((3, rows, half), BF16)] * OWNERS
    out_specs = [pl.BlockSpec((3, rows, LANES), lambda h: (0, 0, h))] * OWNERS
    if not routed:
        inputs.append(chosen)
        specs.append(VMEM_SPEC)
        slots = chosen.shape[1]
        shapes += [jax.ShapeDtypeStruct((3, slots, half), BF16)] * OWNERS
        out_specs += [pl.BlockSpec((3, slots, LANES), lambda h: (0, 0, h))] * OWNERS
    inputs += list(saved) + list(grads)
    specs += [
        pl.BlockSpec((3, length, LANES), lambda h: (0, 0, h)),
        pl.BlockSpec((length, LANES), lambda h: (0, h)),
        pl.BlockSpec((1, 8, length), lambda h: (h, 0, 0)),
    ] + [pl.BlockSpec((rows, LANES), lambda h: (0, h))] * OWNERS
    blocks = length // BLOCK
    work = blocks * (blocks + 1) // 2 * BLOCK * BLOCK * 2 * pairs
    outs = pl.pallas_call(
        lambda *refs: attend_back_kernel(rows, routed, *refs),
        name="attend_routed_back" if routed else "attend_dense_back",
        grid=(pairs,),
        out_shape=shapes,
        in_specs=specs,
        out_specs=out_specs,
        scratch_shapes=[pltpu.VMEM((length, LANES), BF16)]
        + [pltpu.VMEM((length, LANES), F32)] * 3,
        compiler_params=pltpu.CompilerParams(vmem_limit_bytes=VMEM_BYTES),
        cost_estimate=cost(40 * HEAD_DIM * work, 16 * length * half, work),
    )(*inputs)
    return outs[:OWNERS], outs[OWNERS:]


SPARE = 32
Y_STAGE = -1


def send_orders(bits):
    dp = list(range(bits))
    rest = dp[2:]
    return (
        [dp[0], dp[1]] + rest + [Y_STAGE],
        [dp[1], dp[0]] + rest + [Y_STAGE],
        [Y_STAGE, dp[0], dp[1]] + rest,
        [dp[0], Y_STAGE, dp[1]] + rest,
        [dp[1], Y_STAGE, dp[0]] + rest,
    )


def position(order, slab, y_half):
    spot = 0
    for k in order:
        spot = 2 * spot + (y_half if k == Y_STAGE else ((slab >> k) & 1))
    return spot


def store_slabs(target, bits, place, first, found, rows):
    ref, at, which = target
    order = send_orders(bits)[which]
    part = rows // 2
    for d in range(found.shape[0] // rows):
        for y_half in range(2):
            spot = position(order, first + d, y_half) ^ place[2 + which]
            low = d * rows + y_half * part
            ref[pl.ds(spot, 1), at // 2 : at // 2 + part, :] = found[low : low + part].astype(
                BF16
            )[None]


def feed_grad_kernel(bits, orders, routed, place, *refs):
    ff_refs, gel_refs, mix_refs, gh_refs, gff_refs, gatt_refs = (
        refs[2 * k : 2 * k + 2] for k in range(6)
    )
    refs = refs[12:]
    width = ff_refs[0].shape[1]
    half = width // 2
    slabs = 1 << bits
    narrow = width // slabs
    wide = OWNERS * narrow
    first, second = refs[-2:]
    if routed:
        for d in range(slabs):
            store_slabs((first, wide, orders[0]), bits, place, d, refs[0][d], SPARE)
    own = pl.ds(pl.multiple_of(place[1] * half, LANES), half)
    turned = [ref[...].T for ref in ff_refs]
    for t in range(OWNERS):
        tile = pl.ds(pl.multiple_of((place[1] * OWNERS + t) * half, LANES), half)
        found = dot(turned[0], gh_refs[0][:, tile])
        found = found + dot(turned[1], gh_refs[1][:, t * half : (t + 1) * half])
        store_slabs((first, t * narrow, orders[0]), bits, place, 0, found, narrow)
    for t in range(OWNERS):
        rows = slice(t * width, (t + 1) * width)
        found = dot(gel_refs[0][:, rows], gff_refs[0][:, own], TN)
        found = found + dot(gel_refs[1][:, rows], gff_refs[1][...], TN)
        store_slabs((second, 0, orders[1]), bits, place, t * slabs // OWNERS, found, wide)
    found = dot(mix_refs[0][...], gatt_refs[0][:, own], TN)
    found = found + dot(mix_refs[1][...], gatt_refs[1][...], TN)
    store_slabs((second, wide, orders[1]), bits, place, 0, found, narrow)


def feed_grad(place, bits, orders, operands, route=None):
    tokens, width = operands[0].shape
    half = width // 2
    slabs = 1 << bits
    narrow = width // slabs
    wide = OWNERS * narrow
    routed = route is not None
    rows = (wide + (SPARE if routed else 0), wide + narrow)
    extra = [route] if routed else []
    return pl.pallas_call(
        lambda *refs: feed_grad_kernel(bits, orders, routed, *refs),
        name="feed_grad",
        in_specs=[SMEM_SPEC] + [VMEM_SPEC] * (12 + len(extra)),
        out_specs=[VMEM_SPEC] * len(rows),
        out_shape=[jax.ShapeDtypeStruct((2 * slabs, count // 2, half), BF16) for count in rows],
        compiler_params=pltpu.CompilerParams(vmem_limit_bytes=VMEM_BYTES),
        cost_estimate=cost(
            18 * tokens * width * width, 9 * width * width + 40 * tokens * width
        ),
    )(place, *operands, *extra)


def qkv_grad_kernel(bits, order, place, *refs):
    acts, pieces, out = refs[:OWNERS], refs[OWNERS : 2 * OWNERS], refs[2 * OWNERS]
    narrow = acts[0].shape[1] // (1 << bits)
    for part in range(3):
        found = dot(acts[0][...], pieces[0][part], TN)
        for r in range(1, OWNERS):
            found = found + dot(acts[r][...], pieces[r][part], TN)
        store_slabs((out, part * narrow, order), bits, place, 0, found, narrow)


def qkv_grad(place, bits, order, acts, pieces):
    rows, width = acts[0].shape
    half = width // 2
    slabs = 1 << bits
    narrow = width // slabs
    return pl.pallas_call(
        lambda *refs: qkv_grad_kernel(bits, order, *refs),
        name="qkv_grad",
        in_specs=[SMEM_SPEC] + [VMEM_SPEC] * (2 * OWNERS),
        out_specs=VMEM_SPEC,
        out_shape=jax.ShapeDtypeStruct((2 * slabs, 3 * narrow // 2, half), BF16),
        compiler_params=pltpu.CompilerParams(vmem_limit_bytes=VMEM_BYTES),
        cost_estimate=cost(
            12 * rows * width * width, 3 * width * width + 20 * rows * width
        ),
    )(place, *acts, *pieces)


def finish_kernel(down_at, place, near_ref, far_ref, qkv_ref, out_ref, up_ref, down_ref):
    narrow, width = out_ref.shape
    half = width // 2
    wide = OWNERS * narrow

    for flip, ref in ((0, near_ref), (1, far_ref)):
        side = place[1] ^ flip

        def put(out, tile, at, rows):
            columns = pl.ds(pl.multiple_of(tile * half, LANES), half)
            for y_half in range(2):
                part = rows // 2
                out[y_half * part : (y_half + 1) * part, columns] = ref[
                    y_half, at // 2 : at // 2 + part, :
                ].astype(F32)

        for t in range(OWNERS):
            put(up_ref, side * OWNERS + t, t * narrow, narrow)
        put(down_ref, side, down_at, wide)
        put(out_ref, side, down_at + wide, narrow)
        for p in range(3):
            put(qkv_ref, 2 * p + side, down_at + wide + (1 + p) * narrow, narrow)


def finish(place, down_at, narrow, width, near, far):
    shapes = [(narrow, 3 * width), (narrow, width), (narrow, 4 * width), (4 * narrow, width)]
    return pl.pallas_call(
        lambda *refs: finish_kernel(down_at, *refs),
        name="finish_grads",
        in_specs=[SMEM_SPEC] + [VMEM_SPEC] * 2,
        out_specs=[VMEM_SPEC] * 4,
        out_shape=[jax.ShapeDtypeStruct(shape, F32) for shape in shapes],
        compiler_params=pltpu.CompilerParams(vmem_limit_bytes=VMEM_BYTES),
        cost_estimate=cost(0, 72 * narrow * width),
    )(place, near, far)


def swap(x, axis, bit):
    size = lax.axis_size(axis)
    return lax.ppermute(x, axis, [(i, i ^ bit) for i in range(size)])


def exchange(pieces):
    return [pieces[0]] + [swap(pieces[r], "seq", r) for r in range(1, OWNERS)]


def add_low(a, b):
    return (a.astype(F32) + b.astype(F32)).astype(BF16)


def halves(unit):
    n = unit.shape[0] // 2
    return unit[:n], unit[n:]


def combine(keep, received):
    if keep.shape[0] == 1:
        return add_low(keep, received)[0]
    (low, high), (low_in, high_in) = halves(keep), halves(received)
    return add_low(low, low_in), add_low(high, high_in)


def stage_swap(state, order, stage):
    k = order[stage]
    return swap(state[1], "seq", 2) if k == Y_STAGE else swap(state[1], "dp", 1 << k)


class Chain:
    def __init__(self, unit, order):
        self.unit, self.order, self.stage = unit, order, 0
        self.state = None, halves(unit)[1]

    def step(self, after):
        if self.stage == 0:
            unit, _ = hold(self.unit, after)
            keep = halves(unit)[0]
        else:
            keep, _ = hold(self.state[0], after)
        self.state = combine(keep, stage_swap(self.state, self.order, self.stage))
        self.stage += 1
        return self.state


def merge(chains):
    found = Chain.__new__(Chain)
    found.order, found.stage = chains[0].order, chains[0].stage
    found.state = tuple(
        jnp.concatenate([chain.state[k] for chain in chains], axis=1) for k in range(2)
    )
    return found


def advance(chains, stage, token):
    for chain in chains:
        while chain.stage < min(stage, len(chain.order)):
            token = chain.step(token)
    return token


def gather_halves(own, y_first):
    other = swap(own, "seq", 2)
    pair = jnp.stack([jnp.where(y_first, own, other), jnp.where(y_first, other, own)])
    return pair, swap(pair, "seq", 1)


def hold(*values):
    return lax.optimization_barrier(values)


def both_halves(own, other, first):
    return jnp.concatenate(
        [jnp.where(first, own, other), jnp.where(first, other, own)], axis=-1
    )


def assemble(pieces, y_first, core_first):
    near = both_halves(pieces[0], pieces[1], core_first)
    far = both_halves(pieces[2], pieces[3], core_first)
    return jnp.stack([jnp.where(y_first, near, far), jnp.where(y_first, far, near)])


def assemble_packed(pieces, y_first, core_first):
    found = assemble(pieces, y_first, core_first)
    return jnp.concatenate([found[:, 0], found[:, 1], found[:, 2]], axis=-1)


def core_half(x, at):
    half = x.shape[-1] // 2
    return lax.dynamic_slice_in_dim(x, at * half, half, axis=x.ndim - 1)


def with_far(x):
    return x, swap(x, "seq", 1)


def half_with_far(x, core_at):
    return x, swap(core_half(x, 1 - core_at), "seq", 1)


def split_pieces(x, place):
    half = x.shape[-1] // 2
    found = []
    for r in range(OWNERS):
        rows = lax.dynamic_index_in_dim(x, place[0] ^ (r >> 1), 0, keepdims=False)
        found.append(lax.dynamic_slice_in_dim(rows, (place[1] ^ (r & 1)) * half, half, axis=1))
    return found


def norm_rows(vector, gain_vec):
    return (
        vector * lax.rsqrt(jnp.mean(vector * vector, axis=-1, keepdims=True) + EPSILON) * gain_vec
    )


def project(left_side, weight):
    return jnp.einsum("bnd,de->bne", left_side, weight, preferred_element_type=F32)


def project_back(gradient, weight):
    return jnp.einsum("bne,de->bnd", gradient, weight, preferred_element_type=F32)


def feed_forward(resid, router, mixture, w_out, gain_two, w_up, w_down):
    attended = project(mixture, w_out)
    middle = resid + attended if router is None else resid + router[..., None] * attended
    ff_in = norm_rows(middle, gain_two.astype(F32)).astype(BF16)
    hidden = project(ff_in, w_up)
    activated = jax.nn.gelu(hidden).astype(BF16)
    done = middle + project(activated, w_down)
    return done, (attended, middle, ff_in, hidden, activated)


def hidden_backward(grad_done, w_down, hidden):
    grad_ff = grad_done.astype(BF16)
    grad_act = project_back(grad_ff, w_down)
    unused_value, gelu_pull = jax.vjp(jax.nn.gelu, hidden)
    return grad_ff, gelu_pull(grad_act)[0].astype(BF16)


def feed_backward(grad_done, grad_hidden, router, w_out, gain_two, w_up, middle):
    grad_ffin = project_back(grad_hidden, w_up)
    grad_middle = grad_done + norm_back(middle, gain_two, grad_ffin)
    scaled = grad_middle if router is None else router[..., None] * grad_middle
    grad_attended = scaled.astype(BF16)
    grad_mixture = project_back(grad_attended, w_out).astype(BF16)
    return grad_middle, grad_attended, grad_mixture


def norm_back(x, gain, grad_act_in):
    unused, pull = jax.vjp(lambda x: norm_rows(x, gain.astype(F32)), x)
    return pull(grad_act_in)[0]


def per_device(
    stream_in,
    chosen,
    counts,
    route_w,
    gain_a1,
    qkv_a,
    out_a,
    gain_a2,
    up_a,
    down_a,
    gain_b1,
    qkv_b,
    out_b,
    gain_b2,
    up_b,
    down_b,
    cotangent,
):
    seqs, rows, width = stream_in.shape
    slots = chosen.shape[1]
    half = width // 2
    dp_size = lax.axis_size("dp")
    bits = dp_size.bit_length() - 1
    narrow = width // dp_size
    me = lax.axis_index("seq")
    dp_at = lax.axis_index("dp")
    y_at, core_at = me // 2, me % 2
    y_first, core_first = y_at == 0, core_at == 0
    orders = send_orders(bits)
    place = jnp.stack(
        [y_at, core_at] + [position(order, dp_at, y_at) for order in orders]
    ).astype(jnp.int32)
    counts_mine = lax.dynamic_index_in_dim(counts, y_at, 0, keepdims=False)
    own_load = lax.dynamic_index_in_dim(counts, me, 1, keepdims=False)
    live = jnp.arange(slots, dtype=jnp.int32)[None, :] < own_load[:, None]
    hits = chosen[:, :, None] == jnp.arange(rows, dtype=jnp.int32)
    gather = hits.astype(BF16)
    live_hits = (hits & live[..., None]).astype(F32)
    covered = jnp.any(hits & live[..., None], axis=1)[..., None]
    tag = jnp.pad(chosen.astype(BF16), ((0, 0), (0, LANES - slots)))
    tag = jnp.pad(jnp.tile(tag, (1, half // LANES))[:, None, :], ((0, 0), (0, 15), (0, 0)))

    def scatter(values):
        return jnp.einsum("bcr,bcd->brd", live_hits, values, precision=EXACT)

    def flat(x):
        return x.reshape(x.shape[0] * x.shape[1], x.shape[2])

    picked = jnp.einsum("bcr,brd->bcd", gather, stream_in, preferred_element_type=F32)
    picked_low = picked.astype(BF16)
    router = jnp.einsum("bcd,d->bc", picked_low, route_w, preferred_element_type=F32)
    act_a, pieces = project_pieces(place, picked_low, gain_a1, qkv_a)
    pieces = exchange(pieces)
    act_base, base = project_pieces(place, stream_in, gain_b1, qkv_b, tag)
    base_two = swap(base[2], "seq", 2)
    mixed, saved_a = attend(place, counts_mine, slots, pieces)
    mixed = exchange(mixed)
    mixed, late = hold(mixed, (base[1], base[3]))
    base = [base[0], swap(late[0], "seq", 1), base_two, swap(late[1], "seq", 3)]
    mixture_a = assemble(mixed, y_first, core_first)
    done_a, kept_a = feed_forward(picked, router, mixture_a, out_a, gain_a2, up_a, down_a)
    change = jnp.where(live[..., None], done_a - picked, 0.0)
    slot_mid = picked + change
    early_a = [with_far(flat(x)) for x in (kept_a[2], kept_a[4], mixture_a)]
    base_three, early_a, slot_mid = hold(base[3], early_a, slot_mid)
    base = base[:3] + [base_three]
    act_slot, slot_pieces = project_pieces(place, slot_mid, gain_b1, qkv_b)
    slot_pieces = exchange(slot_pieces)
    chosen_mine = jnp.concatenate(
        [piece[0, rows : rows + 1, :slots] for piece in base], axis=0
    ).astype(jnp.int32)
    act_b = jnp.where(
        covered,
        jnp.einsum("bcr,bcd->brd", live_hits.astype(BF16), act_slot, preferred_element_type=F32),
        act_base.astype(F32),
    ).astype(BF16)
    acts = jnp.concatenate([act_b, act_a], axis=1)
    acts_near = lax.dynamic_index_in_dim(acts, y_at, 0, keepdims=False)
    acts_far = lax.dynamic_index_in_dim(acts, 1 - y_at, 0, keepdims=False)
    middle = stream_in.astype(F32) + scatter(change)
    slot_pieces, acts_near, acts_far, middle = hold(slot_pieces, acts_near, acts_far, middle)
    acts_pair = jnp.stack([acts_near, swap(acts_far, "seq", 2)])
    mixed, saved_b = attend(
        place, counts_mine, rows, base, chosen_mine, slot_pieces
    )
    acts_other = swap(acts_pair, "seq", 1)
    acts = [acts_pair[0], acts_other[0], acts_pair[1], acts_other[1]]
    acts_b = [x[:rows] for x in acts]
    acts_a = [x[rows:] for x in acts]
    mixture_b = assemble(exchange(mixed), y_first, core_first)
    done_b, kept_b = feed_forward(middle, None, mixture_b, out_b, gain_b2, up_b, down_b)

    flat_b = [flat(x) for x in (kept_b[2], kept_b[4], mixture_b)]
    early = [with_far(x) for x in flat_b]
    early_grad = half_with_far(flat(cotangent), core_at)
    grad_done_b = cotangent.astype(F32)
    grad_ff_b, grad_hidden_b = hidden_backward(grad_done_b, down_b, kept_b[3])
    grad_mid_b, grad_att_b, grad_mix_b = feed_backward(
        grad_done_b, grad_hidden_b, None, out_b, gain_b2, up_b, kept_b[1]
    )
    grads = split_pieces(grad_mix_b, place)
    late = [half_with_far(flat(x), core_at) for x in (grad_hidden_b, grad_att_b)]
    grads, early = hold(grads, early)
    grads = exchange(grads)
    operands = [y for x in early + [late[0], early_grad, late[1]] for y in x]
    feed_b = feed_grad(place, bits, (0, 1), operands)
    grads, feed_b = hold(grads, feed_b)
    chains_b = [Chain(unit, send_orders(bits)[k]) for k, unit in enumerate(feed_b)]
    packed_b, packed_slot = attend_back(place, counts_mine, saved_b, grads, chosen_mine)
    packed_slot = exchange(packed_slot)
    part_b = qkv_grad(place, bits, 3, acts_b, packed_b)
    token = advance(chains_b, 1, part_b)
    packed_slot, part_b, packed_b, token = hold(packed_slot, part_b, packed_b, token)
    feed_chains_b, part_chain_b = chains_b, Chain(part_b, send_orders(bits)[3])
    packed_two = swap(packed_b[2], "seq", 2)

    grad_packed_slot = assemble_packed(packed_slot, y_first, core_first)
    slot_grad = norm_back(slot_mid, gain_b1, project_back(grad_packed_slot, qkv_b))
    mid_at_slot = jnp.einsum("bcr,brd->bcd", live_hits, grad_mid_b, precision=EXACT)
    grad_done = jnp.where(live[..., None], mid_at_slot + slot_grad, 0.0)
    grad_ff_a, grad_hidden_a = hidden_backward(grad_done, down_a, kept_a[3])
    token = advance(feed_chains_b, 2, (token, grad_hidden_a))
    grad_hidden_a, token = hold(grad_hidden_a, token)
    feed_chain_b = merge(feed_chains_b)
    grad_mid_a, grad_att_a, grad_mix_a = feed_backward(
        grad_done, grad_hidden_a, router, out_a, gain_a2, up_a, kept_a[1]
    )
    grads = split_pieces(grad_mix_a, place)
    late = [
        half_with_far(flat(x), core_at) for x in (grad_hidden_a, grad_ff_a, grad_att_a)
    ]
    grads, packed_two, token = hold(grads, packed_two, token)
    grads = exchange(grads)
    grad_router = jnp.sum(kept_a[0] * grad_mid_a, axis=-1)
    grad_route = jnp.einsum("bc,bcd->d", grad_router, picked, precision=EXACT)
    route = jnp.pad(
        grad_route.reshape(dp_size, 1, narrow), ((0, 0), (0, SPARE - 1), (0, half - narrow))
    )
    operands = [y for x in early_a + late for y in x]
    feed_a = feed_grad(place, bits, (3, 2), operands, route)
    token = advance([part_chain_b], 1, (token, feed_a))
    grads, feed_a, late, token = hold(grads, feed_a, (packed_b[1], packed_b[3]), token)
    packed_three = swap(late[1], "seq", 3)
    up_chain_a = Chain(feed_a[0], send_orders(bits)[3])
    packed_a, _ = attend_back(place, counts_mine, saved_a, grads)
    returned_a = exchange(packed_a)
    part_a = qkv_grad(place, bits, 4, acts_a, packed_a)
    returned_a, part_a, down_a_unit, packed_three, token = hold(
        returned_a, part_a, feed_a[1], packed_three, token
    )
    returned_b = [packed_b[0], swap(late[0], "seq", 1), packed_two, packed_three]
    down_chain_a = Chain(down_a_unit, send_orders(bits)[2])
    part_chain_a = Chain(part_a, send_orders(bits)[4])
    chains_a = [up_chain_a, down_chain_a, part_chain_a]

    grad_packed_a = assemble_packed(returned_a, y_first, core_first)
    res_a = norm_back(picked, gain_a1, project_back(grad_packed_a, qkv_a))
    grad_picked = (
        grad_mid_a + res_a + grad_router[..., None] * route_w.astype(F32) - grad_done
    )
    token = advance([up_chain_a], 1, (token, grad_picked))
    token = advance([feed_chain_b], bits, token)
    token = advance([part_chain_b], 2, token)
    token = advance([down_chain_a, part_chain_a], 1, token)
    done_b, returned_b, token = hold(done_b, returned_b, token)
    token = advance(chains_a, 2, token)
    token = advance([feed_chain_b], bits + 1, token)
    token = advance([part_chain_b], 3, token)
    token = advance(chains_a, 3, token)
    token = advance([part_chain_b], bits + 1, token)
    near_b, far_b = gather_halves(
        jnp.concatenate([feed_chain_b.state, part_chain_b.state]), y_first
    )
    token = advance(chains_a, bits, token)

    grad_packed_b = assemble_packed(returned_b, y_first, core_first)
    res_b = norm_back(middle, gain_b1, project_back(grad_packed_b, qkv_b))
    grad_input = grad_mid_b + res_b + scatter(grad_picked)
    qkv_gb, out_gb, up_gb, down_gb = finish(place, OWNERS * narrow, narrow, width, near_b, far_b)
    token = advance(chains_a, bits + 1, token)
    near, far = gather_halves(jnp.concatenate([x.state for x in chains_a]), y_first)
    down_at = OWNERS * narrow + SPARE
    qkv_ga, out_ga, up_ga, down_ga = finish(place, down_at, narrow, width, near, far)
    at = OWNERS * narrow // 2
    route = near[0, at, :narrow].astype(F32) + far[0, at, :narrow].astype(F32)

    def gain_grad(found, weight, gain):
        at = dp_at * narrow
        weight = lax.dynamic_slice_in_dim(weight, at, narrow, axis=0).astype(F32)
        gain = lax.dynamic_slice_in_dim(gain, at, narrow, axis=0).astype(F32)
        return jnp.sum(found * weight, axis=1) / gain

    return (
        done_b.astype(BF16),
        grad_input,
        route,
        gain_grad(qkv_ga, qkv_a, gain_a1),
        qkv_ga,
        out_ga,
        gain_grad(up_ga, up_a, gain_a2),
        up_ga,
        down_ga,
        gain_grad(qkv_gb, qkv_b, gain_b1),
        qkv_gb,
        out_gb,
        gain_grad(up_gb, up_b, gain_b2),
        up_gb,
        down_gb,
    )


def solution(mesh):
    tokens, whole, shared = P("dp", "seq", None), P(), P("dp")
    weights = P("dp", None)
    return jax.shard_map(
        per_device,
        mesh=mesh,
        in_specs=(tokens, P("dp", "seq"), P("dp", None)) + (whole,) * 13 + (tokens,),
        out_specs=(tokens, tokens, shared)
        + (shared, weights, weights, shared, weights, weights) * 2,
        check_vma=False,
    )
```

```python
import jax
import jax.numpy as jnp
from jax import lax
from jax.experimental import pallas as pl
from jax.experimental.pallas import tpu as pltpu
from jax.sharding import PartitionSpec as P

HEADS = 12
HEAD_DIM = 64
EPSILON = 1e-06
EXACT = lax.Precision.HIGHEST
F32 = jnp.float32
BF16 = jnp.bfloat16
OWNERS = 4
LANES = 128
BLOCK = 256
VMEM_BYTES = 60 * 1024 * 1024

SMEM_SPEC = pl.BlockSpec(memory_space=pltpu.SMEM)
VMEM_SPEC = pl.BlockSpec(memory_space=pltpu.VMEM)
NT = (((1,), (1,)), ((), ()))
TN = (((0,), (0,)), ((), ()))


def dot(left, right, dims=(((1,), (0,)), ((), ()))):
    return lax.dot_general(left, right, dims, preferred_element_type=F32)


def cost(flops, moved, exps=0):
    return pl.CostEstimate(flops=int(flops), bytes_accessed=int(moved), transcendentals=int(exps))


def project_kernel(tagged, place, x_ref, gain_ref, w_ref, *refs):
    tag_ref, refs = (refs[0], refs[1:]) if tagged else (None, refs)
    act_ref, outs = refs[0], refs[1:]
    rows, width = x_ref.shape[1:]
    half = width // 2
    gain = gain_ref[...].astype(F32).reshape(1, width)
    for i in range(2):
        x = x_ref[i].astype(F32)
        scale = lax.rsqrt(jnp.mean(x * x, axis=-1, keepdims=True) + EPSILON)
        act_ref[i] = (x * scale * gain).astype(BF16)
    for r in (3, 2, 1, 0):
        act = act_ref[place[0] ^ (r >> 1)]
        at = (place[1] ^ (r & 1)) * half
        for part in range(3):
            columns = pl.ds(pl.multiple_of(part * width + at, LANES), half)
            outs[r][part, :rows, :] = dot(act, w_ref[:, columns]).astype(BF16)
            if tagged:
                outs[r][part, rows:, :] = tag_ref[place[0] ^ (r >> 1)]


def project_pieces(place, x, gain, weight, tag=None):
    seqs, rows, width = x.shape
    tagged = tag is not None
    extra = [tag] if tagged else []
    spare = tag.shape[1] if tagged else 0
    piece = jax.ShapeDtypeStruct((3, rows + spare, width // 2), BF16)
    outs = pl.pallas_call(
        lambda *refs: project_kernel(tagged, *refs),
        name="project_pieces",
        out_shape=[jax.ShapeDtypeStruct(x.shape, BF16)] + [piece] * OWNERS,
        in_specs=[SMEM_SPEC] + [VMEM_SPEC] * (3 + len(extra)),
        out_specs=[VMEM_SPEC] * (1 + OWNERS),
        compiler_params=pltpu.CompilerParams(vmem_limit_bytes=VMEM_BYTES),
        cost_estimate=cost(
            2 * seqs * rows * width * 3 * width, 6 * width * width + 12 * seqs * rows * width
        ),
    )(place, x, gain, weight, *extra)
    return outs[0], outs[1:]


def lane_head(head):
    lanes = lax.broadcasted_iota(jnp.int32, (1, LANES), 1)
    return (lanes < HEAD_DIM) if head == 0 else (lanes >= HEAD_DIM)


def only_head(x, head):
    return jnp.where(lane_head(head), x, jnp.zeros_like(x))


def slot_matrix(chosen_ref, counts, r, owner, rows):
    slots = chosen_ref.shape[1]
    spots = chosen_ref[r : r + 1, :]
    row_ids = lax.broadcasted_iota(jnp.int32, (rows, slots), 0)
    slot_ids = lax.broadcasted_iota(jnp.int32, (rows, slots), 1)
    return jnp.where((row_ids == spots) & (slot_ids < counts[owner]), 1.0, 0.0)


def diagonal_mask(counts, query_axis, rows, routed):
    shape = (BLOCK, BLOCK)
    queries = lax.broadcasted_iota(jnp.int32, shape, query_axis)
    keys = lax.broadcasted_iota(jnp.int32, shape, 1 - query_axis)
    if not routed:
        return keys <= queries
    owner = keys // rows
    load = jnp.where(
        owner == 0,
        counts[0],
        jnp.where(owner == 1, counts[1], jnp.where(owner == 2, counts[2], counts[3])),
    )
    live = (keys - owner * rows) < load
    return (keys == queries) | ((keys < queries) & live)


def attend_kernel(rows, routed, place, counts, *refs):
    if routed:
        base, refs = refs[:OWNERS], refs[OWNERS:]
    else:
        chosen_ref, base, slot_in = refs[0], refs[1 : 1 + OWNERS], refs[1 + OWNERS : 1 + 2 * OWNERS]
        refs = refs[1 + 2 * OWNERS :]
    outs, (merged, mixed, stats) = refs[:OWNERS], refs[OWNERS:]
    me = 2 * place[0] + place[1]
    blocks = OWNERS * rows // BLOCK
    for r in range(OWNERS):
        owner = me ^ r
        at = pl.ds(pl.multiple_of(owner * rows, rows), rows)
        if routed:
            for part in range(3):
                merged[part, at, :] = base[r][part]
        else:
            spots = slot_matrix(chosen_ref, counts, r, owner, rows)
            covered = jnp.max(spots, axis=1, keepdims=True) > 0.5
            spots = spots.astype(BF16)
            for part in range(3):
                placed = dot(spots, slot_in[r][part])
                merged[part, at, :] = jnp.where(
                    covered, placed, base[r][part].astype(F32)
                ).astype(BF16)
    visible = diagonal_mask(counts, 0, rows, routed)
    for a in range(blocks):
        queries = merged[0, a * BLOCK : (a + 1) * BLOCK, :] * jnp.asarray(HEAD_DIM**-0.5, BF16)
        mixture = jnp.zeros((BLOCK, LANES), F32)
        stat = jnp.zeros((BLOCK, LANES), F32)
        for head in range(2):
            own = only_head(queries, head)
            scores = []
            for b in range(a + 1):
                keys = merged[1, b * BLOCK : (b + 1) * BLOCK, :]
                found = dot(own, keys, NT)
                scores.append(jnp.where(visible, found, -1e30) if b == a else found)
            top = scores[0]
            for found in scores[1:]:
                top = jnp.maximum(top, found)
            top = jnp.max(top, axis=1, keepdims=True)
            part = jnp.zeros((BLOCK, LANES), F32)
            for b in range(a + 1):
                weight = jnp.exp(scores[b] - top).astype(BF16)
                values = merged[2, b * BLOCK : (b + 1) * BLOCK, :]
                part = part + dot(weight, jnp.where(lane_head(head), values, jnp.ones_like(values)))
            turned = pltpu.roll(part, HEAD_DIM, axis=1)
            mixture = jnp.where(lane_head(head), part * (1.0 / turned), mixture)
            total = turned if head == 0 else part
            lane = lax.broadcasted_iota(jnp.int32, (1, LANES), 1)
            stat = jnp.where(lane == head, top + jnp.log(total), stat)
        mixed[a * BLOCK : (a + 1) * BLOCK, :] = mixture.astype(BF16)
        stats[0, :, a * BLOCK : (a + 1) * BLOCK] = stat.T[:8, :]
    for r in range(OWNERS):
        at = pl.ds(pl.multiple_of((me ^ r) * rows, rows), rows)
        outs[r][...] = mixed[at, :]


def attend(place, counts, rows, base, chosen=None, slots=None):
    routed = slots is None
    half = base[0].shape[2]
    pairs = half // LANES
    length = OWNERS * rows
    inputs = [place, counts]
    specs = [SMEM_SPEC, SMEM_SPEC]
    if not routed:
        inputs.append(chosen)
        specs.append(VMEM_SPEC)
    for group, count in ((base, rows), (slots, None if routed else chosen.shape[1])):
        if group is not None:
            inputs += list(group)
            specs += [pl.BlockSpec((3, count, LANES), lambda h: (0, 0, h))] * OWNERS
    blocks = length // BLOCK
    work = blocks * (blocks + 1) // 2 * BLOCK * BLOCK * 2 * pairs
    outs = pl.pallas_call(
        lambda *refs: attend_kernel(rows, routed, *refs),
        name="attend_routed" if routed else "attend_dense",
        grid=(pairs,),
        out_shape=[jax.ShapeDtypeStruct((rows, half), BF16)] * OWNERS
        + [
            jax.ShapeDtypeStruct((3, length, half), BF16),
            jax.ShapeDtypeStruct((length, half), BF16),
            jax.ShapeDtypeStruct((pairs, 8, length), F32),
        ],
        in_specs=specs,
        out_specs=[pl.BlockSpec((rows, LANES), lambda h: (0, h))] * OWNERS
        + [
            pl.BlockSpec((3, length, LANES), lambda h: (0, 0, h)),
            pl.BlockSpec((length, LANES), lambda h: (0, h)),
            pl.BlockSpec((1, 8, length), lambda h: (h, 0, 0)),
        ],
        compiler_params=pltpu.CompilerParams(vmem_limit_bytes=VMEM_BYTES),
        cost_estimate=cost(16 * HEAD_DIM * work, 16 * length * half, work),
    )(*inputs)
    return outs[:OWNERS], outs[OWNERS:]


def attend_back_kernel(rows, routed, place, counts, *refs):
    if not routed:
        chosen_ref, refs = refs[0], refs[1:]
    merged, mixed, stats, grads = refs[0], refs[1], refs[2], refs[3 : 3 + OWNERS]
    outs, refs = refs[3 + OWNERS : 3 + 2 * OWNERS], refs[3 + 2 * OWNERS :]
    if not routed:
        slot_outs, refs = refs[:OWNERS], refs[OWNERS:]
    incoming, turned_keys, grad_q, grad_k, grad_v = refs
    turned_keys[...] = merged[1].T
    me = 2 * place[0] + place[1]
    blocks = OWNERS * rows // BLOCK
    for r in range(OWNERS):
        at = pl.ds(pl.multiple_of((me ^ r) * rows, rows), rows)
        incoming[at, :] = grads[r][...]
    for ref in (grad_q, grad_k, grad_v):
        ref[...] = jnp.zeros_like(ref)
    visible = diagonal_mask(counts, 1, rows, routed)
    for a in range(blocks):
        span = slice(a * BLOCK, (a + 1) * BLOCK)
        queries = merged[0, span, :] * jnp.asarray(HEAD_DIM**-0.5, BF16)
        grad_mix = incoming[span, :]
        grad_queries = []
        inner = (grad_mix.astype(F32) * mixed[span, :].astype(F32)).T
        for head in range(2):
            own_q = only_head(queries, head)
            own_g = only_head(grad_mix, head)
            level = stats[0, head : head + 1, span]
            head_rows = slice(head * HEAD_DIM, (head + 1) * HEAD_DIM)
            grad_query = jnp.zeros((HEAD_DIM, BLOCK), F32)
            offset = jnp.sum(inner[head_rows], axis=0, keepdims=True)
            for b in range(a + 1):
                keys_at = slice(b * BLOCK, (b + 1) * BLOCK)
                prob = jnp.exp(dot(merged[1, keys_at, :], own_q, NT) - level)
                if b == a:
                    prob = jnp.where(visible, prob, 0.0)
                grad_prob = dot(merged[2, keys_at, :], own_g, NT)
                grad_v[keys_at, :] += dot(prob.astype(BF16), own_g)
                grad_score = (prob * (grad_prob - offset)).astype(BF16)
                grad_k[keys_at, :] += dot(grad_score, own_q)
                grad_query = grad_query + dot(turned_keys[head_rows, keys_at], grad_score)
            grad_queries.append(grad_query)
        grad_q[span, :] = jnp.concatenate(grad_queries, axis=0).T * HEAD_DIM**-0.5
    for r in range(OWNERS):
        owner = me ^ r
        at = pl.ds(pl.multiple_of(owner * rows, rows), rows)
        if not routed:
            spots = slot_matrix(chosen_ref, counts, r, owner, rows).astype(BF16)
        for part, ref in enumerate((grad_q, grad_k, grad_v)):
            found = ref[at, :].astype(BF16)
            outs[r][part] = found
            if not routed:
                slot_outs[r][part] = dot(spots, found, TN).astype(BF16)


def attend_back(place, counts, saved, grads, chosen=None):
    routed = chosen is None
    rows, half = grads[0].shape
    pairs = half // LANES
    length = OWNERS * rows
    inputs = [place, counts]
    specs = [SMEM_SPEC, SMEM_SPEC]
    shapes = [jax.ShapeDtypeStruct((3, rows, half), BF16)] * OWNERS
    out_specs = [pl.BlockSpec((3, rows, LANES), lambda h: (0, 0, h))] * OWNERS
    if not routed:
        inputs.append(chosen)
        specs.append(VMEM_SPEC)
        slots = chosen.shape[1]
        shapes += [jax.ShapeDtypeStruct((3, slots, half), BF16)] * OWNERS
        out_specs += [pl.BlockSpec((3, slots, LANES), lambda h: (0, 0, h))] * OWNERS
    inputs += list(saved) + list(grads)
    specs += [
        pl.BlockSpec((3, length, LANES), lambda h: (0, 0, h)),
        pl.BlockSpec((length, LANES), lambda h: (0, h)),
        pl.BlockSpec((1, 8, length), lambda h: (h, 0, 0)),
    ] + [pl.BlockSpec((rows, LANES), lambda h: (0, h))] * OWNERS
    blocks = length // BLOCK
    work = blocks * (blocks + 1) // 2 * BLOCK * BLOCK * 2 * pairs
    outs = pl.pallas_call(
        lambda *refs: attend_back_kernel(rows, routed, *refs),
        name="attend_routed_back" if routed else "attend_dense_back",
        grid=(pairs,),
        out_shape=shapes,
        in_specs=specs,
        out_specs=out_specs,
        scratch_shapes=[
            pltpu.VMEM((length, LANES), BF16),
            pltpu.VMEM((LANES, length), BF16),
        ]
        + [pltpu.VMEM((length, LANES), F32)] * 3,
        compiler_params=pltpu.CompilerParams(vmem_limit_bytes=VMEM_BYTES),
        cost_estimate=cost(40 * HEAD_DIM * work, 16 * length * half, work),
    )(*inputs)
    return outs[:OWNERS], outs[OWNERS:]


SPARE = 32
Y_STAGE = -1


def send_orders(bits):
    dp = list(range(bits))
    rest = dp[2:]
    return (
        [dp[0], Y_STAGE, dp[1]] + rest,
        [dp[1], dp[0], Y_STAGE] + rest,
        [Y_STAGE, dp[1], dp[0]] + rest,
    )


def position(order, slab, y_half):
    spot = 0
    for k in order:
        spot = 2 * spot + (y_half if k == Y_STAGE else ((slab >> k) & 1))
    return spot


def store_slabs(target, bits, place, first, found, rows):
    ref, at, which = target
    order = send_orders(bits)[which]
    part = rows // 2
    for d in range(found.shape[0] // rows):
        for y_half in range(2):
            spot = position(order, first + d, y_half) ^ place[2 + which]
            low = d * rows + y_half * part
            ref[pl.ds(spot, 1), at // 2 : at // 2 + part, :] = found[low : low + part].astype(
                BF16
            )[None]


def start_halves(unit, keep, send, sems):
    n = keep.shape[0]
    copies = [
        pltpu.make_async_copy(unit.at[pl.ds(0, n)], keep, sems.at[0]),
        pltpu.make_async_copy(unit.at[pl.ds(n, n)], send, sems.at[1]),
    ]
    for copy in copies:
        copy.start()
    return copies


def halves_out(slabs, rows, half):
    return [jax.ShapeDtypeStruct((slabs, rows // 2, half), BF16)] * 2


def unit_scratch(slabs, rows, half):
    return [pltpu.VMEM((2 * slabs, rows // 2, half), BF16), pltpu.SemaphoreType.DMA((2,))]


ANY_SPEC = pl.BlockSpec(memory_space=pl.ANY)


def feed_grad_kernel(bits, orders, routed, place, *refs):
    ff_refs, gel_refs, mix_refs, gh_refs, gff_refs, gatt_refs = (
        refs[2 * k : 2 * k + 2] for k in range(6)
    )
    refs = refs[12:]
    width = ff_refs[0].shape[1]
    half = width // 2
    slabs = 1 << bits
    narrow = width // slabs
    wide = OWNERS * narrow
    first, first_sems, second, second_sems = refs[-4:]
    outs = refs[-8:-4]
    if routed:
        for d in range(slabs):
            store_slabs((first, wide, orders[0]), bits, place, d, refs[0][d], SPARE)
    own = pl.ds(pl.multiple_of(place[1] * half, LANES), half)
    turned = [ref[...].T for ref in ff_refs]
    for t in range(OWNERS):
        tile = pl.ds(pl.multiple_of((place[1] * OWNERS + t) * half, LANES), half)
        found = dot(turned[0], gh_refs[0][:, tile])
        found = found + dot(turned[1], gh_refs[1][:, t * half : (t + 1) * half])
        store_slabs((first, t * narrow, orders[0]), bits, place, 0, found, narrow)
    copies = start_halves(first, outs[0], outs[1], first_sems)
    for t in range(OWNERS):
        rows = slice(t * width, (t + 1) * width)
        found = dot(gel_refs[0][:, rows], gff_refs[0][:, own], TN)
        found = found + dot(gel_refs[1][:, rows], gff_refs[1][...], TN)
        store_slabs((second, 0, orders[1]), bits, place, t * slabs // OWNERS, found, wide)
    found = dot(mix_refs[0][...], gatt_refs[0][:, own], TN)
    found = found + dot(mix_refs[1][...], gatt_refs[1][...], TN)
    store_slabs((second, wide, orders[1]), bits, place, 0, found, narrow)
    for copy in copies + start_halves(second, outs[2], outs[3], second_sems):
        copy.wait()


def feed_grad(place, bits, orders, operands, route=None):
    tokens, width = operands[0].shape
    half = width // 2
    slabs = 1 << bits
    narrow = width // slabs
    wide = OWNERS * narrow
    routed = route is not None
    rows = (wide + (SPARE if routed else 0), wide + narrow)
    extra = [route] if routed else []
    up_keep, up_send, down_keep, down_send = pl.pallas_call(
        lambda *refs: feed_grad_kernel(bits, orders, routed, *refs),
        name="feed_grad",
        in_specs=[SMEM_SPEC] + [VMEM_SPEC] * (12 + len(extra)),
        out_specs=[ANY_SPEC] * 4,
        out_shape=halves_out(slabs, rows[0], half) + halves_out(slabs, rows[1], half),
        scratch_shapes=unit_scratch(slabs, rows[0], half) + unit_scratch(slabs, rows[1], half),
        compiler_params=pltpu.CompilerParams(vmem_limit_bytes=VMEM_BYTES),
        cost_estimate=cost(
            18 * tokens * width * width, 9 * width * width + 40 * tokens * width
        ),
    )(place, *operands, *extra)
    return (up_keep, up_send), (down_keep, down_send)


def qkv_grad_kernel(bits, order, place, *refs):
    acts, pieces = refs[:OWNERS], refs[OWNERS : 2 * OWNERS]
    keep, send, out, sems = refs[2 * OWNERS :]
    narrow = acts[0].shape[1] // (1 << bits)
    for part in range(3):
        found = dot(acts[0][...], pieces[0][part], TN)
        for r in range(1, OWNERS):
            found = found + dot(acts[r][...], pieces[r][part], TN)
        store_slabs((out, part * narrow, order), bits, place, 0, found, narrow)
    for copy in start_halves(out, keep, send, sems):
        copy.wait()


def qkv_grad(place, bits, order, acts, pieces):
    rows, width = acts[0].shape
    half = width // 2
    slabs = 1 << bits
    narrow = width // slabs
    return pl.pallas_call(
        lambda *refs: qkv_grad_kernel(bits, order, *refs),
        name="qkv_grad",
        in_specs=[SMEM_SPEC] + [VMEM_SPEC] * (2 * OWNERS),
        out_specs=[ANY_SPEC] * 2,
        out_shape=halves_out(slabs, 3 * narrow, half),
        scratch_shapes=unit_scratch(slabs, 3 * narrow, half),
        compiler_params=pltpu.CompilerParams(vmem_limit_bytes=VMEM_BYTES),
        cost_estimate=cost(
            12 * rows * width * width, 3 * width * width + 20 * rows * width
        ),
    )(place, *acts, *pieces)


def finish_kernel(down_at, place, near_ref, far_ref, qkv_ref, out_ref, up_ref, down_ref):
    narrow, width = out_ref.shape
    half = width // 2
    wide = OWNERS * narrow

    for flip, ref in ((0, near_ref), (1, far_ref)):
        side = place[1] ^ flip

        def put(out, tile, at, rows):
            columns = pl.ds(pl.multiple_of(tile * half, LANES), half)
            for y_half in range(2):
                part = rows // 2
                out[y_half * part : (y_half + 1) * part, columns] = ref[
                    y_half, at // 2 : at // 2 + part, :
                ].astype(F32)

        for t in range(OWNERS):
            put(up_ref, side * OWNERS + t, t * narrow, narrow)
        put(down_ref, side, down_at, wide)
        put(out_ref, side, down_at + wide, narrow)
        for p in range(3):
            put(qkv_ref, 2 * p + side, down_at + wide + (1 + p) * narrow, narrow)


def finish(place, down_at, narrow, width, near, far):
    shapes = [(narrow, 3 * width), (narrow, width), (narrow, 4 * width), (4 * narrow, width)]
    return pl.pallas_call(
        lambda *refs: finish_kernel(down_at, *refs),
        name="finish_grads",
        in_specs=[SMEM_SPEC] + [VMEM_SPEC] * 2,
        out_specs=[VMEM_SPEC] * 4,
        out_shape=[jax.ShapeDtypeStruct(shape, F32) for shape in shapes],
        compiler_params=pltpu.CompilerParams(vmem_limit_bytes=VMEM_BYTES),
        cost_estimate=cost(0, 72 * narrow * width),
    )(place, near, far)


def swap(x, axis, bit):
    size = lax.axis_size(axis)
    return lax.ppermute(x, axis, [(i, i ^ bit) for i in range(size)])


def exchange(pieces):
    return [pieces[0]] + [swap(pieces[r], "seq", r) for r in range(1, OWNERS)]


def add_low(a, b):
    return (a.astype(F32) + b.astype(F32)).astype(BF16)


def halves(unit):
    n = unit.shape[0] // 2
    return unit[:n], unit[n:]


def combine(keep, received):
    if keep.shape[0] == 1:
        return add_low(keep, received)[0]
    (low, high), (low_in, high_in) = halves(keep), halves(received)
    return add_low(low, low_in), add_low(high, high_in)


def stage_swap(state, order, stage):
    k = order[stage]
    return swap(state[1], "seq", 2) if k == Y_STAGE else swap(state[1], "dp", 1 << k)


class Chain:
    def __init__(self, unit, order):
        self.state, self.order, self.stage = unit, order, 0

    def step(self):
        received = stage_swap(self.state, self.order, self.stage)
        self.state = combine(self.state[0], received)
        self.stage += 1

    @property
    def done(self):
        return self.stage == len(self.order)


def merge(chains):
    found = Chain.__new__(Chain)
    found.order, found.stage = chains[0].order, chains[0].stage
    found.state = tuple(
        jnp.concatenate([chain.state[k] for chain in chains], axis=1) for k in range(2)
    )
    return found


def meet(chains, *values):
    held = hold([chain.state for chain in chains], *values)
    for chain, state in zip(chains, held[0]):
        chain.state = state
    return held[1:]


def stage(chains, *values):
    for chain in chains:
        chain.step()
    return meet(chains, *values)


def gather_halves(own, y_first):
    other = swap(own, "seq", 2)
    pair = jnp.stack([jnp.where(y_first, own, other), jnp.where(y_first, other, own)])
    return pair, swap(pair, "seq", 1)


def hold(*values):
    return lax.optimization_barrier(values)


def both_halves(own, other, first):
    return jnp.concatenate(
        [jnp.where(first, own, other), jnp.where(first, other, own)], axis=-1
    )


def assemble(pieces, y_first, core_first):
    near = both_halves(pieces[0], pieces[1], core_first)
    far = both_halves(pieces[2], pieces[3], core_first)
    return jnp.stack([jnp.where(y_first, near, far), jnp.where(y_first, far, near)])


def assemble_packed(pieces, y_first, core_first):
    found = assemble(pieces, y_first, core_first)
    return jnp.concatenate([found[:, 0], found[:, 1], found[:, 2]], axis=-1)


def core_half(x, at):
    half = x.shape[-1] // 2
    return lax.dynamic_slice_in_dim(x, at * half, half, axis=x.ndim - 1)


def with_far(x):
    return x, swap(x, "seq", 1)


def half_with_far(x, core_at):
    return x, swap(core_half(x, 1 - core_at), "seq", 1)


def split_pieces(x, place):
    half = x.shape[-1] // 2
    found = []
    for r in range(OWNERS):
        rows = lax.dynamic_index_in_dim(x, place[0] ^ (r >> 1), 0, keepdims=False)
        found.append(lax.dynamic_slice_in_dim(rows, (place[1] ^ (r & 1)) * half, half, axis=1))
    return found


def norm_rows(vector, gain_vec):
    return (
        vector * lax.rsqrt(jnp.mean(vector * vector, axis=-1, keepdims=True) + EPSILON) * gain_vec
    )


def project(left_side, weight):
    return jnp.einsum("bnd,de->bne", left_side, weight, preferred_element_type=F32)


def project_back(gradient, weight):
    return jnp.einsum("bne,de->bnd", gradient, weight, preferred_element_type=F32)


def feed_forward(resid, router, mixture, w_out, gain_two, w_up, w_down):
    attended = project(mixture, w_out)
    middle = resid + attended if router is None else resid + router[..., None] * attended
    ff_in = norm_rows(middle, gain_two.astype(F32)).astype(BF16)
    hidden = project(ff_in, w_up)
    activated = jax.nn.gelu(hidden).astype(BF16)
    done = middle + project(activated, w_down)
    return done, (attended, middle, ff_in, hidden, activated)


def hidden_backward(grad_done, w_down, hidden):
    grad_ff = grad_done.astype(BF16)
    grad_act = project_back(grad_ff, w_down)
    unused_value, gelu_pull = jax.vjp(jax.nn.gelu, hidden)
    return grad_ff, gelu_pull(grad_act)[0].astype(BF16)


def feed_backward(grad_done, grad_hidden, router, w_out, gain_two, w_up, middle):
    grad_ffin = project_back(grad_hidden, w_up)
    grad_middle = grad_done + norm_back(middle, gain_two, grad_ffin)
    scaled = grad_middle if router is None else router[..., None] * grad_middle
    grad_attended = scaled.astype(BF16)
    grad_mixture = project_back(grad_attended, w_out).astype(BF16)
    return grad_middle, grad_attended, grad_mixture


def norm_back(x, gain, grad_act_in):
    unused, pull = jax.vjp(lambda x: norm_rows(x, gain.astype(F32)), x)
    return pull(grad_act_in)[0]


def per_device(
    stream_in,
    chosen,
    counts,
    route_w,
    gain_a1,
    qkv_a,
    out_a,
    gain_a2,
    up_a,
    down_a,
    gain_b1,
    qkv_b,
    out_b,
    gain_b2,
    up_b,
    down_b,
    cotangent,
):
    seqs, rows, width = stream_in.shape
    slots = chosen.shape[1]
    half = width // 2
    dp_size = lax.axis_size("dp")
    bits = dp_size.bit_length() - 1
    narrow = width // dp_size
    me = lax.axis_index("seq")
    dp_at = lax.axis_index("dp")
    y_at, core_at = me // 2, me % 2
    y_first, core_first = y_at == 0, core_at == 0
    orders = send_orders(bits)
    place = jnp.stack(
        [y_at, core_at] + [position(order, dp_at, y_at) for order in orders]
    ).astype(jnp.int32)
    counts_mine = lax.dynamic_index_in_dim(counts, y_at, 0, keepdims=False)
    own_load = lax.dynamic_index_in_dim(counts, me, 1, keepdims=False)
    live = jnp.arange(slots, dtype=jnp.int32)[None, :] < own_load[:, None]
    hits = chosen[:, :, None] == jnp.arange(rows, dtype=jnp.int32)
    gather = hits.astype(BF16)
    live_hits = (hits & live[..., None]).astype(F32)
    covered = jnp.any(hits & live[..., None], axis=1)[..., None]
    tag = jnp.pad(chosen.astype(BF16), ((0, 0), (0, LANES - slots)))
    tag = jnp.pad(jnp.tile(tag, (1, half // LANES))[:, None, :], ((0, 0), (0, 15), (0, 0)))

    def scatter(values):
        return jnp.einsum("bcr,bcd->brd", live_hits, values, precision=EXACT)

    def flat(x):
        return x.reshape(x.shape[0] * x.shape[1], x.shape[2])

    picked = jnp.einsum("bcr,brd->bcd", gather, stream_in, preferred_element_type=F32)
    picked_low = picked.astype(BF16)
    router = jnp.einsum("bcd,d->bc", picked_low, route_w, preferred_element_type=F32)
    act_a, pieces = project_pieces(place, picked_low, gain_a1, qkv_a)
    pieces = exchange(pieces)
    act_base, base = project_pieces(place, stream_in, gain_b1, qkv_b, tag)
    base_two = swap(base[2], "seq", 2)
    mixed, saved_a = attend(place, counts_mine, slots, pieces)
    mixed = exchange(mixed)
    mixed, late = hold(mixed, (base[1], base[3]))
    base = [base[0], swap(late[0], "seq", 1), base_two, swap(late[1], "seq", 3)]
    mixture_a = assemble(mixed, y_first, core_first)
    done_a, kept_a = feed_forward(picked, router, mixture_a, out_a, gain_a2, up_a, down_a)
    change = jnp.where(live[..., None], done_a - picked, 0.0)
    slot_mid = picked + change
    early_a = [with_far(flat(x)) for x in (kept_a[2], kept_a[4], mixture_a)]
    base_three, early_a, slot_mid = hold(base[3], early_a, slot_mid)
    base = base[:3] + [base_three]
    act_slot, slot_pieces = project_pieces(place, slot_mid, gain_b1, qkv_b)
    slot_pieces = exchange(slot_pieces)
    chosen_mine = jnp.concatenate(
        [piece[0, rows : rows + 1, :slots] for piece in base], axis=0
    ).astype(jnp.int32)
    act_b = jnp.where(
        covered,
        jnp.einsum("bcr,bcd->brd", live_hits.astype(BF16), act_slot, preferred_element_type=F32),
        act_base.astype(F32),
    ).astype(BF16)
    acts = jnp.concatenate([act_b, act_a], axis=1)
    acts_near = lax.dynamic_index_in_dim(acts, y_at, 0, keepdims=False)
    acts_far = lax.dynamic_index_in_dim(acts, 1 - y_at, 0, keepdims=False)
    middle = stream_in.astype(F32) + scatter(change)
    slot_pieces, acts_near, acts_far, middle = hold(slot_pieces, acts_near, acts_far, middle)
    acts_pair = jnp.stack([acts_near, swap(acts_far, "seq", 2)])
    mixed, saved_b = attend(
        place, counts_mine, rows, base, chosen_mine, slot_pieces
    )
    acts_other = swap(acts_pair, "seq", 1)
    acts = [acts_pair[0], acts_other[0], acts_pair[1], acts_other[1]]
    acts_b = [x[:rows] for x in acts]
    acts_a = [x[rows:] for x in acts]
    mixture_b = assemble(exchange(mixed), y_first, core_first)
    done_b, kept_b = feed_forward(middle, None, mixture_b, out_b, gain_b2, up_b, down_b)

    flat_b = [flat(x) for x in (kept_b[2], kept_b[4], mixture_b)]
    early = [with_far(x) for x in flat_b]
    early_grad = half_with_far(flat(cotangent), core_at)
    grad_done_b = cotangent.astype(F32)
    grad_ff_b, grad_hidden_b = hidden_backward(grad_done_b, down_b, kept_b[3])
    grad_mid_b, grad_att_b, grad_mix_b = feed_backward(
        grad_done_b, grad_hidden_b, None, out_b, gain_b2, up_b, kept_b[1]
    )
    grads = split_pieces(grad_mix_b, place)
    late = [half_with_far(flat(x), core_at) for x in (grad_hidden_b, grad_att_b)]
    grads, early = hold(grads, early)
    grads = exchange(grads)
    operands = [y for x in early + [late[0], early_grad, late[1]] for y in x]
    feed_b = feed_grad(place, bits, (0, 1), operands)
    grads, feed_b = hold(grads, feed_b)
    x_order, z_order, y_order = send_orders(bits)
    feed_chains_b = [Chain(unit, order) for unit, order in zip(feed_b, (x_order, z_order))]
    packed_b, packed_slot = attend_back(place, counts_mine, saved_b, grads, chosen_mine)
    packed_slot = exchange(packed_slot)
    part_chain_b = Chain(qkv_grad(place, bits, 0, acts_b, packed_b), x_order)
    packed_slot, packed_b, _ = stage(feed_chains_b, packed_slot, packed_b, part_chain_b.state)

    grad_packed_slot = assemble_packed(packed_slot, y_first, core_first)
    slot_grad = norm_back(slot_mid, gain_b1, project_back(grad_packed_slot, qkv_b))
    mid_at_slot = jnp.einsum("bcr,brd->bcd", live_hits, grad_mid_b, precision=EXACT)
    grad_done = jnp.where(live[..., None], mid_at_slot + slot_grad, 0.0)
    grad_ff_a, grad_hidden_a = hidden_backward(grad_done, down_a, kept_a[3])
    (grad_hidden_a,) = stage(feed_chains_b, grad_hidden_a)
    (grad_hidden_a,) = meet([part_chain_b], grad_hidden_a)
    grad_mid_a, grad_att_a, grad_mix_a = feed_backward(
        grad_done, grad_hidden_a, router, out_a, gain_a2, up_a, kept_a[1]
    )
    grads = split_pieces(grad_mix_a, place)
    late = [
        half_with_far(flat(x), core_at) for x in (grad_hidden_a, grad_ff_a, grad_att_a)
    ]
    grads = exchange(grads)
    grad_router = jnp.sum(kept_a[0] * grad_mid_a, axis=-1)
    grad_route = jnp.einsum("bc,bcd->d", grad_router, picked, precision=EXACT)
    route = jnp.pad(
        grad_route.reshape(dp_size, 1, narrow), ((0, 0), (0, SPARE - 1), (0, half - narrow))
    )
    operands = [y for x in early_a + late for y in x]
    feed_a = feed_grad(place, bits, (0, 1), operands, route)
    grads, feed_a = stage(feed_chains_b + [part_chain_b], grads, feed_a)
    part_chain_b.step()
    feed_chain_b = merge(feed_chains_b)
    feed_chains_a = [Chain(unit, order) for unit, order in zip(feed_a, (x_order, z_order))]
    packed_a, _ = attend_back(place, counts_mine, saved_a, grads)
    (packed_a,) = meet([part_chain_b], packed_a)
    returned_a = exchange(packed_a)
    part_chain_a = Chain(qkv_grad(place, bits, 2, acts_a, packed_a), y_order)
    returned_a, packed_b, kept_last = meet([part_chain_a], returned_a, packed_b, kept_b[4])
    done_b = kept_b[1] + project(kept_last, down_b)
    gains = [
        lax.dynamic_slice_in_dim(gain, dp_at * narrow, narrow, axis=0).astype(F32)
        for gain in (gain_a1, gain_a2, gain_b1, gain_b2)
    ]

    grad_packed_a = assemble_packed(returned_a, y_first, core_first)
    res_a = norm_back(picked, gain_a1, project_back(grad_packed_a, qkv_a))
    grad_picked = (
        grad_mid_a + res_a + grad_router[..., None] * route_w.astype(F32) - grad_done
    )
    late_weight, packed_b = hold(qkv_b, packed_b)
    weight_parts = [
        lax.dynamic_slice_in_dim(late_weight, part * width + core_at * half, half, axis=1)
        for part in range(3)
    ]
    shares = [
        sum(dot(piece[part], weight_parts[part], NT) for part in range(3)) for piece in packed_b
    ]
    tail = feed_chains_a + [part_chain_a]
    b_side = [feed_chain_b, part_chain_b]
    for chain in tail:
        chain.step()
    given = swap(jnp.stack([shares[1].astype(BF16), shares[3].astype(BF16)]), "seq", 1)
    act_near = shares[0] + given[0].astype(F32)
    act_far = (shares[2] + given[1].astype(F32)).astype(BF16)
    grad_picked, act_near, act_far, done_b, gains = meet(
        tail + b_side, grad_picked, act_near, act_far, done_b, gains
    )
    for chain in b_side:
        chain.step()
    stage(tail)
    meet(b_side, tail[0].state)
    if not part_chain_b.done:
        part_chain_b.step()
    (act_far,) = stage(tail, act_far)
    act_far = swap(act_far, "seq", 2).astype(F32)
    last = merge(tail)
    for chain in [last] + b_side:
        while not chain.done:
            chain.step()
    def gain_grad(found, weight, gain):
        at = dp_at * narrow
        weight = lax.dynamic_slice_in_dim(weight, at, narrow, axis=0).astype(F32)
        return jnp.sum(found * weight, axis=1) / gain

    near_b, far_b = gather_halves(
        jnp.concatenate([feed_chain_b.state, part_chain_b.state]), y_first
    )

    grad_act_b = jnp.stack(
        [jnp.where(y_first, act_near, act_far), jnp.where(y_first, act_far, act_near)]
    )
    res_b = norm_back(middle, gain_b1, grad_act_b)
    grad_input = grad_mid_b + res_b + scatter(grad_picked)
    qkv_gb, out_gb, up_gb, down_gb = finish(place, OWNERS * narrow, narrow, width, near_b, far_b)
    own = last.state
    gains_b = gain_grad(qkv_gb, qkv_b, gains[2]), gain_grad(up_gb, up_b, gains[3])
    other, gains_b, _ = hold(
        swap(own, "seq", 2), gains_b, (qkv_gb, out_gb, up_gb, down_gb, grad_input)
    )
    near = jnp.stack([jnp.where(y_first, own, other), jnp.where(y_first, other, own)])
    far = swap(near, "seq", 1)
    down_at = OWNERS * narrow + SPARE
    qkv_ga, out_ga, up_ga, down_ga = finish(place, down_at, narrow, width, near, far)
    at = OWNERS * narrow // 2
    route = near[0, at, :narrow].astype(F32) + far[0, at, :narrow].astype(F32)

    return (
        done_b.astype(BF16),
        grad_input,
        route,
        gain_grad(qkv_ga, qkv_a, gains[0]),
        qkv_ga,
        out_ga,
        gain_grad(up_ga, up_a, gains[1]),
        up_ga,
        down_ga,
        gains_b[0],
        qkv_gb,
        out_gb,
        gains_b[1],
        up_gb,
        down_gb,
    )


def solution(mesh):
    tokens, whole, shared = P("dp", "seq", None), P(), P("dp")
    weights = P("dp", None)
    return jax.shard_map(
        per_device,
        mesh=mesh,
        in_specs=(tokens, P("dp", "seq"), P("dp", None)) + (whole,) * 13 + (tokens,),
        out_specs=(tokens, tokens, shared)
        + (shared, weights, weights, shared, weights, weights) * 2,
        check_vma=False,
    )
```

```python
import jax
import jax.numpy as jnp
from jax import lax
from jax.experimental import pallas as pl
from jax.experimental.pallas import tpu as pltpu
from jax.sharding import PartitionSpec as P

HEADS = 12
HEAD_DIM = 64
EPSILON = 1e-06
EXACT = lax.Precision.HIGHEST
F32 = jnp.float32
BF16 = jnp.bfloat16
OWNERS = 4
LANES = 128
BLOCK = 256
VMEM_BYTES = 60 * 1024 * 1024

SMEM_SPEC = pl.BlockSpec(memory_space=pltpu.SMEM)
VMEM_SPEC = pl.BlockSpec(memory_space=pltpu.VMEM)
NT = (((1,), (1,)), ((), ()))
TN = (((0,), (0,)), ((), ()))


def dot(left, right, dims=(((1,), (0,)), ((), ()))):
    return lax.dot_general(left, right, dims, preferred_element_type=F32)


def cost(flops, moved, exps=0):
    return pl.CostEstimate(flops=int(flops), bytes_accessed=int(moved), transcendentals=int(exps))


def project_kernel(tagged, place, x_ref, gain_ref, w_ref, *refs):
    tag_ref, refs = (refs[0], refs[1:]) if tagged else (None, refs)
    act_ref, outs = refs[0], refs[1:]
    rows, width = x_ref.shape[1:]
    half = width // 2
    gain = gain_ref[...].astype(F32).reshape(1, width)
    for i in range(2):
        x = x_ref[i].astype(F32)
        scale = lax.rsqrt(jnp.mean(x * x, axis=-1, keepdims=True) + EPSILON)
        act_ref[i] = (x * scale * gain).astype(BF16)
    for r in (3, 2, 1, 0):
        act = act_ref[place[0] ^ (r >> 1)]
        at = (place[1] ^ (r & 1)) * half
        for part in range(3):
            columns = pl.ds(pl.multiple_of(part * width + at, LANES), half)
            outs[r][part, :rows, :] = dot(act, w_ref[:, columns]).astype(BF16)
            if tagged:
                outs[r][part, rows:, :] = tag_ref[place[0] ^ (r >> 1)]


def project_pieces(place, x, gain, weight, tag=None):
    seqs, rows, width = x.shape
    tagged = tag is not None
    extra = [tag] if tagged else []
    spare = tag.shape[1] if tagged else 0
    piece = jax.ShapeDtypeStruct((3, rows + spare, width // 2), BF16)
    outs = pl.pallas_call(
        lambda *refs: project_kernel(tagged, *refs),
        name="project_pieces",
        out_shape=[jax.ShapeDtypeStruct(x.shape, BF16)] + [piece] * OWNERS,
        in_specs=[SMEM_SPEC] + [VMEM_SPEC] * (3 + len(extra)),
        out_specs=[VMEM_SPEC] * (1 + OWNERS),
        compiler_params=pltpu.CompilerParams(vmem_limit_bytes=VMEM_BYTES),
        cost_estimate=cost(
            2 * seqs * rows * width * 3 * width, 6 * width * width + 12 * seqs * rows * width
        ),
    )(place, x, gain, weight, *extra)
    return outs[0], outs[1:]


def lane_head(head):
    lanes = lax.broadcasted_iota(jnp.int32, (1, LANES), 1)
    return (lanes < HEAD_DIM) if head == 0 else (lanes >= HEAD_DIM)


def only_head(x, head):
    return jnp.where(lane_head(head), x, jnp.zeros_like(x))


def slot_matrix(chosen_ref, counts, r, owner, rows):
    slots = chosen_ref.shape[1]
    spots = chosen_ref[r : r + 1, :]
    row_ids = lax.broadcasted_iota(jnp.int32, (rows, slots), 0)
    slot_ids = lax.broadcasted_iota(jnp.int32, (rows, slots), 1)
    return jnp.where((row_ids == spots) & (slot_ids < counts[owner]), 1.0, 0.0)


def diagonal_mask(counts, query_axis, rows, routed):
    shape = (BLOCK, BLOCK)
    queries = lax.broadcasted_iota(jnp.int32, shape, query_axis)
    keys = lax.broadcasted_iota(jnp.int32, shape, 1 - query_axis)
    if not routed:
        return keys <= queries
    owner = keys // rows
    load = jnp.where(
        owner == 0,
        counts[0],
        jnp.where(owner == 1, counts[1], jnp.where(owner == 2, counts[2], counts[3])),
    )
    live = (keys - owner * rows) < load
    return (keys == queries) | ((keys < queries) & live)


def attend_kernel(rows, routed, place, counts, *refs):
    if routed:
        base, refs = refs[:OWNERS], refs[OWNERS:]
    else:
        chosen_ref, base, slot_in = refs[0], refs[1 : 1 + OWNERS], refs[1 + OWNERS : 1 + 2 * OWNERS]
        refs = refs[1 + 2 * OWNERS :]
    outs, (merged, mixed, stats) = refs[:OWNERS], refs[OWNERS:]
    me = 2 * place[0] + place[1]
    blocks = OWNERS * rows // BLOCK
    for r in range(OWNERS):
        owner = me ^ r
        at = pl.ds(pl.multiple_of(owner * rows, rows), rows)
        if routed:
            for part in range(3):
                merged[part, at, :] = base[r][part]
        else:
            spots = slot_matrix(chosen_ref, counts, r, owner, rows)
            covered = jnp.max(spots, axis=1, keepdims=True) > 0.5
            spots = spots.astype(BF16)
            for part in range(3):
                placed = dot(spots, slot_in[r][part])
                merged[part, at, :] = jnp.where(
                    covered, placed, base[r][part].astype(F32)
                ).astype(BF16)
    visible = diagonal_mask(counts, 0, rows, routed)
    for a in range(blocks):
        queries = merged[0, a * BLOCK : (a + 1) * BLOCK, :] * jnp.asarray(HEAD_DIM**-0.5, BF16)
        mixture = jnp.zeros((BLOCK, LANES), F32)
        stat = jnp.zeros((BLOCK, LANES), F32)
        for head in range(2):
            own = only_head(queries, head)
            scores = []
            for b in range(a + 1):
                keys = merged[1, b * BLOCK : (b + 1) * BLOCK, :]
                found = dot(own, keys, NT)
                scores.append(jnp.where(visible, found, -1e30) if b == a else found)
            top = scores[0]
            for found in scores[1:]:
                top = jnp.maximum(top, found)
            top = jnp.max(top, axis=1, keepdims=True)
            part = jnp.zeros((BLOCK, LANES), F32)
            for b in range(a + 1):
                weight = jnp.exp(scores[b] - top).astype(BF16)
                values = merged[2, b * BLOCK : (b + 1) * BLOCK, :]
                part = part + dot(weight, jnp.where(lane_head(head), values, jnp.ones_like(values)))
            turned = pltpu.roll(part, HEAD_DIM, axis=1)
            mixture = jnp.where(lane_head(head), part * (1.0 / turned), mixture)
            total = turned if head == 0 else part
            lane = lax.broadcasted_iota(jnp.int32, (1, LANES), 1)
            stat = jnp.where(lane == head, top + jnp.log(total), stat)
        mixed[a * BLOCK : (a + 1) * BLOCK, :] = mixture.astype(BF16)
        stats[0, :, a * BLOCK : (a + 1) * BLOCK] = stat.T[:8, :]
    for r in range(OWNERS):
        at = pl.ds(pl.multiple_of((me ^ r) * rows, rows), rows)
        outs[r][...] = mixed[at, :]


def attend(place, counts, rows, base, chosen=None, slots=None):
    routed = slots is None
    half = base[0].shape[2]
    pairs = half // LANES
    length = OWNERS * rows
    inputs = [place, counts]
    specs = [SMEM_SPEC, SMEM_SPEC]
    if not routed:
        inputs.append(chosen)
        specs.append(VMEM_SPEC)
    for group, count in ((base, rows), (slots, None if routed else chosen.shape[1])):
        if group is not None:
            inputs += list(group)
            specs += [pl.BlockSpec((3, count, LANES), lambda h: (0, 0, h))] * OWNERS
    blocks = length // BLOCK
    work = blocks * (blocks + 1) // 2 * BLOCK * BLOCK * 2 * pairs
    outs = pl.pallas_call(
        lambda *refs: attend_kernel(rows, routed, *refs),
        name="attend_routed" if routed else "attend_dense",
        grid=(pairs,),
        out_shape=[jax.ShapeDtypeStruct((rows, half), BF16)] * OWNERS
        + [
            jax.ShapeDtypeStruct((3, length, half), BF16),
            jax.ShapeDtypeStruct((length, half), BF16),
            jax.ShapeDtypeStruct((pairs, 8, length), F32),
        ],
        in_specs=specs,
        out_specs=[pl.BlockSpec((rows, LANES), lambda h: (0, h))] * OWNERS
        + [
            pl.BlockSpec((3, length, LANES), lambda h: (0, 0, h)),
            pl.BlockSpec((length, LANES), lambda h: (0, h)),
            pl.BlockSpec((1, 8, length), lambda h: (h, 0, 0)),
        ],
        compiler_params=pltpu.CompilerParams(vmem_limit_bytes=VMEM_BYTES),
        cost_estimate=cost(16 * HEAD_DIM * work, 16 * length * half, work),
    )(*inputs)
    return outs[:OWNERS], outs[OWNERS:]


def attend_back_kernel(rows, routed, place, counts, *refs):
    if not routed:
        chosen_ref, refs = refs[0], refs[1:]
    merged, mixed, stats, grads = refs[0], refs[1], refs[2], refs[3 : 3 + OWNERS]
    outs, refs = refs[3 + OWNERS : 3 + 2 * OWNERS], refs[3 + 2 * OWNERS :]
    if not routed:
        slot_outs, refs = refs[:OWNERS], refs[OWNERS:]
    incoming, turned_keys, grad_q, grad_k, grad_v = refs
    turned_keys[...] = merged[1].T
    me = 2 * place[0] + place[1]
    blocks = OWNERS * rows // BLOCK
    for r in range(OWNERS):
        at = pl.ds(pl.multiple_of((me ^ r) * rows, rows), rows)
        incoming[at, :] = grads[r][...]
    for ref in (grad_q, grad_k, grad_v):
        ref[...] = jnp.zeros_like(ref)
    visible = diagonal_mask(counts, 1, rows, routed)
    for a in range(blocks):
        span = slice(a * BLOCK, (a + 1) * BLOCK)
        queries = merged[0, span, :] * jnp.asarray(HEAD_DIM**-0.5, BF16)
        grad_mix = incoming[span, :]
        grad_queries = []
        inner = (grad_mix.astype(F32) * mixed[span, :].astype(F32)).T
        for head in range(2):
            own_q = only_head(queries, head)
            own_g = only_head(grad_mix, head)
            level = stats[0, head : head + 1, span]
            head_rows = slice(head * HEAD_DIM, (head + 1) * HEAD_DIM)
            grad_query = jnp.zeros((HEAD_DIM, BLOCK), F32)
            offset = jnp.sum(inner[head_rows], axis=0, keepdims=True)
            for b in range(a + 1):
                keys_at = slice(b * BLOCK, (b + 1) * BLOCK)
                prob = jnp.exp(dot(merged[1, keys_at, :], own_q, NT) - level)
                if b == a:
                    prob = jnp.where(visible, prob, 0.0)
                grad_prob = dot(merged[2, keys_at, :], own_g, NT)
                grad_v[keys_at, :] += dot(prob.astype(BF16), own_g)
                grad_score = (prob * (grad_prob - offset)).astype(BF16)
                grad_k[keys_at, :] += dot(grad_score, own_q)
                grad_query = grad_query + dot(turned_keys[head_rows, keys_at], grad_score)
            grad_queries.append(grad_query)
        grad_q[span, :] = jnp.concatenate(grad_queries, axis=0).T * HEAD_DIM**-0.5
    for r in range(OWNERS):
        owner = me ^ r
        at = pl.ds(pl.multiple_of(owner * rows, rows), rows)
        if not routed:
            spots = slot_matrix(chosen_ref, counts, r, owner, rows).astype(BF16)
        for part, ref in enumerate((grad_q, grad_k, grad_v)):
            found = ref[at, :].astype(BF16)
            outs[r][part] = found
            if not routed:
                slot_outs[r][part] = dot(spots, found, TN).astype(BF16)


def attend_back(place, counts, saved, grads, chosen=None):
    routed = chosen is None
    rows, half = grads[0].shape
    pairs = half // LANES
    length = OWNERS * rows
    inputs = [place, counts]
    specs = [SMEM_SPEC, SMEM_SPEC]
    shapes = [jax.ShapeDtypeStruct((3, rows, half), BF16)] * OWNERS
    out_specs = [pl.BlockSpec((3, rows, LANES), lambda h: (0, 0, h))] * OWNERS
    if not routed:
        inputs.append(chosen)
        specs.append(VMEM_SPEC)
        slots = chosen.shape[1]
        shapes += [jax.ShapeDtypeStruct((3, slots, half), BF16)] * OWNERS
        out_specs += [pl.BlockSpec((3, slots, LANES), lambda h: (0, 0, h))] * OWNERS
    inputs += list(saved) + list(grads)
    specs += [
        pl.BlockSpec((3, length, LANES), lambda h: (0, 0, h)),
        pl.BlockSpec((length, LANES), lambda h: (0, h)),
        pl.BlockSpec((1, 8, length), lambda h: (h, 0, 0)),
    ] + [pl.BlockSpec((rows, LANES), lambda h: (0, h))] * OWNERS
    blocks = length // BLOCK
    work = blocks * (blocks + 1) // 2 * BLOCK * BLOCK * 2 * pairs
    outs = pl.pallas_call(
        lambda *refs: attend_back_kernel(rows, routed, *refs),
        name="attend_routed_back" if routed else "attend_dense_back",
        grid=(pairs,),
        out_shape=shapes,
        in_specs=specs,
        out_specs=out_specs,
        scratch_shapes=[
            pltpu.VMEM((length, LANES), BF16),
            pltpu.VMEM((LANES, length), BF16),
        ]
        + [pltpu.VMEM((length, LANES), F32)] * 3,
        compiler_params=pltpu.CompilerParams(vmem_limit_bytes=VMEM_BYTES),
        cost_estimate=cost(40 * HEAD_DIM * work, 16 * length * half, work),
    )(*inputs)
    return outs[:OWNERS], outs[OWNERS:]


SPARE = 32
Y_STAGE = -1


def send_orders(bits):
    dp = list(range(bits))
    rest = dp[2:]
    return (
        [dp[0], Y_STAGE, dp[1]] + rest,
        [dp[1], dp[0], Y_STAGE] + rest,
        [Y_STAGE, dp[1], dp[0]] + rest,
    )


def position(order, slab, y_half):
    spot = 0
    for k in order:
        spot = 2 * spot + (y_half if k == Y_STAGE else ((slab >> k) & 1))
    return spot


def store_slabs(target, bits, place, first, found, rows):
    ref, at, which = target
    order = send_orders(bits)[which]
    part = rows // 2
    for d in range(found.shape[0] // rows):
        for y_half in range(2):
            spot = position(order, first + d, y_half) ^ place[2 + which]
            low = d * rows + y_half * part
            ref[pl.ds(spot, 1), at // 2 : at // 2 + part, :] = found[low : low + part].astype(
                BF16
            )[None]


def start_halves(unit, keep, send, sems):
    n = keep.shape[0]
    copies = [
        pltpu.make_async_copy(unit.at[pl.ds(0, n)], keep, sems.at[0]),
        pltpu.make_async_copy(unit.at[pl.ds(n, n)], send, sems.at[1]),
    ]
    for copy in copies:
        copy.start()
    return copies


def halves_out(slabs, rows, half):
    return [jax.ShapeDtypeStruct((slabs, rows // 2, half), BF16)] * 2


def unit_scratch(slabs, rows, half):
    return [pltpu.VMEM((2 * slabs, rows // 2, half), BF16), pltpu.SemaphoreType.DMA((2,))]


ANY_SPEC = pl.BlockSpec(memory_space=pl.ANY)


def feed_grad_kernel(bits, orders, routed, place, *refs):
    ff_refs, gel_refs, mix_refs, gh_refs, gff_refs, gatt_refs = (
        refs[2 * k : 2 * k + 2] for k in range(6)
    )
    refs = refs[12:]
    width = ff_refs[0].shape[1]
    half = width // 2
    slabs = 1 << bits
    narrow = width // slabs
    wide = OWNERS * narrow
    first, first_sems, second, second_sems = refs[-4:]
    outs = refs[-8:-4]
    if routed:
        for d in range(slabs):
            store_slabs((first, wide, orders[0]), bits, place, d, refs[0][d], SPARE)
    own = pl.ds(pl.multiple_of(place[1] * half, LANES), half)
    turned = [ref[...].T for ref in ff_refs]
    for t in range(OWNERS):
        tile = pl.ds(pl.multiple_of((place[1] * OWNERS + t) * half, LANES), half)
        found = dot(turned[0], gh_refs[0][:, tile])
        found = found + dot(turned[1], gh_refs[1][:, t * half : (t + 1) * half])
        store_slabs((first, t * narrow, orders[0]), bits, place, 0, found, narrow)
    copies = start_halves(first, outs[0], outs[1], first_sems)
    for t in range(OWNERS):
        rows = slice(t * width, (t + 1) * width)
        found = dot(gel_refs[0][:, rows], gff_refs[0][:, own], TN)
        found = found + dot(gel_refs[1][:, rows], gff_refs[1][...], TN)
        store_slabs((second, 0, orders[1]), bits, place, t * slabs // OWNERS, found, wide)
    found = dot(mix_refs[0][...], gatt_refs[0][:, own], TN)
    found = found + dot(mix_refs[1][...], gatt_refs[1][...], TN)
    store_slabs((second, wide, orders[1]), bits, place, 0, found, narrow)
    for copy in copies + start_halves(second, outs[2], outs[3], second_sems):
        copy.wait()


def feed_grad(place, bits, orders, operands, route=None):
    tokens, width = operands[0].shape
    half = width // 2
    slabs = 1 << bits
    narrow = width // slabs
    wide = OWNERS * narrow
    routed = route is not None
    rows = (wide + (SPARE if routed else 0), wide + narrow)
    extra = [route] if routed else []
    up_keep, up_send, down_keep, down_send = pl.pallas_call(
        lambda *refs: feed_grad_kernel(bits, orders, routed, *refs),
        name="feed_grad",
        in_specs=[SMEM_SPEC] + [VMEM_SPEC] * (12 + len(extra)),
        out_specs=[ANY_SPEC] * 4,
        out_shape=halves_out(slabs, rows[0], half) + halves_out(slabs, rows[1], half),
        scratch_shapes=unit_scratch(slabs, rows[0], half) + unit_scratch(slabs, rows[1], half),
        compiler_params=pltpu.CompilerParams(vmem_limit_bytes=VMEM_BYTES),
        cost_estimate=cost(
            18 * tokens * width * width, 9 * width * width + 40 * tokens * width
        ),
    )(place, *operands, *extra)
    return (up_keep, up_send), (down_keep, down_send)


def qkv_grad_kernel(bits, order, place, *refs):
    (pair, other), pieces = refs[:2], refs[2 : 2 + OWNERS]
    keep, send, out, sems = refs[2 + OWNERS :]
    acts = (pair.at[0], other.at[0], pair.at[1], other.at[1])
    narrow = pair.shape[2] // (1 << bits)
    for part in range(3):
        found = dot(acts[0][...], pieces[0][part], TN)
        for r in range(1, OWNERS):
            found = found + dot(acts[r][...], pieces[r][part], TN)
        store_slabs((out, part * narrow, order), bits, place, 0, found, narrow)
    for copy in start_halves(out, keep, send, sems):
        copy.wait()


def qkv_grad(place, bits, order, acts, at, pieces):
    rows, width = pieces[0].shape[1], acts[0].shape[2]
    half = width // 2
    slabs = 1 << bits
    narrow = width // slabs
    return pl.pallas_call(
        lambda *refs: qkv_grad_kernel(bits, order, *refs),
        name="qkv_grad",
        grid=(1,),
        in_specs=[SMEM_SPEC]
        + [pl.BlockSpec((2, rows, width), lambda i: (0, at // rows, 0))] * 2
        + [VMEM_SPEC] * OWNERS,
        out_specs=[ANY_SPEC] * 2,
        out_shape=halves_out(slabs, 3 * narrow, half),
        scratch_shapes=unit_scratch(slabs, 3 * narrow, half),
        compiler_params=pltpu.CompilerParams(vmem_limit_bytes=VMEM_BYTES),
        cost_estimate=cost(
            12 * rows * width * width, 3 * width * width + 20 * rows * width
        ),
    )(place, *acts, *pieces)


def finish_kernel(down_at, place, near_ref, far_ref, qkv_ref, out_ref, up_ref, down_ref):
    narrow, width = out_ref.shape
    half = width // 2
    wide = OWNERS * narrow

    for flip, ref in ((0, near_ref), (1, far_ref)):
        side = place[1] ^ flip

        def put(out, tile, at, rows):
            columns = pl.ds(pl.multiple_of(tile * half, LANES), half)
            for y_half in range(2):
                part = rows // 2
                out[y_half * part : (y_half + 1) * part, columns] = ref[
                    y_half, at // 2 : at // 2 + part, :
                ].astype(F32)

        for t in range(OWNERS):
            put(up_ref, side * OWNERS + t, t * narrow, narrow)
        put(down_ref, side, down_at, wide)
        put(out_ref, side, down_at + wide, narrow)
        for p in range(3):
            put(qkv_ref, 2 * p + side, down_at + wide + (1 + p) * narrow, narrow)


def finish(place, down_at, narrow, width, near, far):
    shapes = [(narrow, 3 * width), (narrow, width), (narrow, 4 * width), (4 * narrow, width)]
    return pl.pallas_call(
        lambda *refs: finish_kernel(down_at, *refs),
        name="finish_grads",
        in_specs=[SMEM_SPEC] + [VMEM_SPEC] * 2,
        out_specs=[VMEM_SPEC] * 4,
        out_shape=[jax.ShapeDtypeStruct(shape, F32) for shape in shapes],
        compiler_params=pltpu.CompilerParams(vmem_limit_bytes=VMEM_BYTES),
        cost_estimate=cost(0, 72 * narrow * width),
    )(place, near, far)


def swap(x, axis, bit):
    size = lax.axis_size(axis)
    return lax.ppermute(x, axis, [(i, i ^ bit) for i in range(size)])


def exchange(pieces):
    return [pieces[0]] + [swap(pieces[r], "seq", r) for r in range(1, OWNERS)]


def add_low(a, b):
    return (a.astype(F32) + b.astype(F32)).astype(BF16)


def halves(unit):
    n = unit.shape[0] // 2
    return unit[:n], unit[n:]


def combine(keep, received):
    if keep.shape[0] == 1:
        return add_low(keep, received)[0]
    (low, high), (low_in, high_in) = halves(keep), halves(received)
    return add_low(low, low_in), add_low(high, high_in)


def stage_swap(state, order, stage):
    k = order[stage]
    return swap(state[1], "seq", 2) if k == Y_STAGE else swap(state[1], "dp", 1 << k)


class Chain:
    def __init__(self, unit, order):
        self.state, self.order, self.stage = unit, order, 0

    def step(self):
        received = stage_swap(self.state, self.order, self.stage)
        self.state = combine(self.state[0], received)
        self.stage += 1

    @property
    def done(self):
        return self.stage == len(self.order)


def merge(chains):
    found = Chain.__new__(Chain)
    found.order, found.stage = chains[0].order, chains[0].stage
    found.state = tuple(
        jnp.concatenate([chain.state[k] for chain in chains], axis=1) for k in range(2)
    )
    return found


def meet(chains, *values):
    held = hold([chain.state for chain in chains], *values)
    for chain, state in zip(chains, held[0]):
        chain.state = state
    return held[1:]


def stage(chains, *values):
    for chain in chains:
        chain.step()
    return meet(chains, *values)


def gather_halves(own, y_first):
    other = swap(own, "seq", 2)
    pair = jnp.stack([jnp.where(y_first, own, other), jnp.where(y_first, other, own)])
    return pair, swap(pair, "seq", 1)


def hold(*values):
    return lax.optimization_barrier(values)


def both_halves(own, other, first):
    return jnp.concatenate(
        [jnp.where(first, own, other), jnp.where(first, other, own)], axis=-1
    )


def assemble(pieces, y_first, core_first):
    near = both_halves(pieces[0], pieces[1], core_first)
    far = both_halves(pieces[2], pieces[3], core_first)
    return jnp.stack([jnp.where(y_first, near, far), jnp.where(y_first, far, near)])


def assemble_packed(pieces, y_first, core_first):
    found = assemble(pieces, y_first, core_first)
    return jnp.concatenate([found[:, 0], found[:, 1], found[:, 2]], axis=-1)


def core_half(x, at):
    half = x.shape[-1] // 2
    return lax.dynamic_slice_in_dim(x, at * half, half, axis=x.ndim - 1)


def with_far(x):
    return x, swap(x, "seq", 1)


def half_with_far(x, core_at):
    return x, swap(core_half(x, 1 - core_at), "seq", 1)


def split_pieces(x, place):
    half = x.shape[-1] // 2
    found = []
    for r in range(OWNERS):
        rows = lax.dynamic_index_in_dim(x, place[0] ^ (r >> 1), 0, keepdims=False)
        found.append(lax.dynamic_slice_in_dim(rows, (place[1] ^ (r & 1)) * half, half, axis=1))
    return found


def norm_rows(vector, gain_vec):
    return (
        vector * lax.rsqrt(jnp.mean(vector * vector, axis=-1, keepdims=True) + EPSILON) * gain_vec
    )


def project(left_side, weight):
    return jnp.einsum("bnd,de->bne", left_side, weight, preferred_element_type=F32)


def project_back(gradient, weight):
    return jnp.einsum("bne,de->bnd", gradient, weight, preferred_element_type=F32)


def feed_forward(resid, router, mixture, w_out, gain_two, w_up, w_down):
    attended = project(mixture, w_out)
    middle = resid + attended if router is None else resid + router[..., None] * attended
    ff_in = norm_rows(middle, gain_two.astype(F32)).astype(BF16)
    hidden = project(ff_in, w_up)
    activated = jax.nn.gelu(hidden).astype(BF16)
    done = middle + project(activated, w_down)
    return done, (attended, middle, ff_in, hidden, activated)


def hidden_backward(grad_done, w_down, hidden):
    grad_ff = grad_done.astype(BF16)
    grad_act = project_back(grad_ff, w_down)
    unused_value, gelu_pull = jax.vjp(jax.nn.gelu, hidden)
    return grad_ff, gelu_pull(grad_act)[0].astype(BF16)


def feed_backward(grad_done, grad_hidden, router, w_out, gain_two, w_up, middle):
    grad_ffin = project_back(grad_hidden, w_up)
    grad_middle = grad_done + norm_back(middle, gain_two, grad_ffin)
    scaled = grad_middle if router is None else router[..., None] * grad_middle
    grad_attended = scaled.astype(BF16)
    grad_mixture = project_back(grad_attended, w_out).astype(BF16)
    return grad_middle, grad_attended, grad_mixture


def norm_back(x, gain, grad_act_in):
    unused, pull = jax.vjp(lambda x: norm_rows(x, gain.astype(F32)), x)
    return pull(grad_act_in)[0]


def per_device(
    stream_in,
    chosen,
    counts,
    route_w,
    gain_a1,
    qkv_a,
    out_a,
    gain_a2,
    up_a,
    down_a,
    gain_b1,
    qkv_b,
    out_b,
    gain_b2,
    up_b,
    down_b,
    cotangent,
):
    seqs, rows, width = stream_in.shape
    slots = chosen.shape[1]
    half = width // 2
    dp_size = lax.axis_size("dp")
    bits = dp_size.bit_length() - 1
    narrow = width // dp_size
    me = lax.axis_index("seq")
    dp_at = lax.axis_index("dp")
    y_at, core_at = me // 2, me % 2
    y_first, core_first = y_at == 0, core_at == 0
    orders = send_orders(bits)
    place = jnp.stack(
        [y_at, core_at] + [position(order, dp_at, y_at) for order in orders]
    ).astype(jnp.int32)
    counts_mine = lax.dynamic_index_in_dim(counts, y_at, 0, keepdims=False)
    own_load = lax.dynamic_index_in_dim(counts, me, 1, keepdims=False)
    live = jnp.arange(slots, dtype=jnp.int32)[None, :] < own_load[:, None]
    hits = chosen[:, :, None] == jnp.arange(rows, dtype=jnp.int32)
    gather = hits.astype(BF16)
    live_hits = (hits & live[..., None]).astype(F32)
    covered = jnp.any(hits & live[..., None], axis=1)[..., None]
    tag = jnp.pad(chosen.astype(BF16), ((0, 0), (0, LANES - slots)))
    tag = jnp.pad(jnp.tile(tag, (1, half // LANES))[:, None, :], ((0, 0), (0, 15), (0, 0)))

    def scatter(values):
        return jnp.einsum("bcr,bcd->brd", live_hits, values, precision=EXACT)

    def flat(x):
        return x.reshape(x.shape[0] * x.shape[1], x.shape[2])

    picked = jnp.einsum("bcr,brd->bcd", gather, stream_in, preferred_element_type=F32)
    picked_low = picked.astype(BF16)
    router = jnp.einsum("bcd,d->bc", picked_low, route_w, preferred_element_type=F32)
    act_a, pieces = project_pieces(place, picked_low, gain_a1, qkv_a)
    pieces = exchange(pieces)
    act_base, base = project_pieces(place, stream_in, gain_b1, qkv_b, tag)
    base_two = swap(base[2], "seq", 2)
    mixed, saved_a = attend(place, counts_mine, slots, pieces)
    mixed = exchange(mixed)
    mixed, late = hold(mixed, (base[1], base[3]))
    base = [base[0], swap(late[0], "seq", 1), base_two, swap(late[1], "seq", 3)]
    mixture_a = assemble(mixed, y_first, core_first)
    done_a, kept_a = feed_forward(picked, router, mixture_a, out_a, gain_a2, up_a, down_a)
    change = jnp.where(live[..., None], done_a - picked, 0.0)
    slot_mid = picked + change
    early_a = [with_far(flat(x)) for x in (kept_a[2], kept_a[4], mixture_a)]
    base_three, early_a, slot_mid = hold(base[3], early_a, slot_mid)
    base = base[:3] + [base_three]
    act_slot, slot_pieces = project_pieces(place, slot_mid, gain_b1, qkv_b)
    slot_pieces = exchange(slot_pieces)
    chosen_mine = jnp.concatenate(
        [piece[0, rows : rows + 1, :slots] for piece in base], axis=0
    ).astype(jnp.int32)
    act_b = jnp.where(
        covered,
        jnp.einsum("bcr,bcd->brd", live_hits.astype(BF16), act_slot, preferred_element_type=F32),
        act_base.astype(F32),
    ).astype(BF16)
    acts = jnp.concatenate([act_b, act_a], axis=1)
    acts_near = lax.dynamic_index_in_dim(acts, y_at, 0, keepdims=False)
    acts_far = lax.dynamic_index_in_dim(acts, 1 - y_at, 0, keepdims=False)
    middle = stream_in.astype(F32) + scatter(change)
    slot_pieces, acts_near, acts_far, middle = hold(slot_pieces, acts_near, acts_far, middle)
    acts_pair = jnp.stack([acts_near, swap(acts_far, "seq", 2)])
    mixed, saved_b = attend(
        place, counts_mine, rows, base, chosen_mine, slot_pieces
    )
    acts_other = swap(acts_pair, "seq", 1)
    acts = (acts_pair, acts_other)
    mixture_b = assemble(exchange(mixed), y_first, core_first)
    done_b, kept_b = feed_forward(middle, None, mixture_b, out_b, gain_b2, up_b, down_b)

    flat_b = [flat(x) for x in (kept_b[2], kept_b[4], mixture_b)]
    early = [with_far(x) for x in flat_b]
    early_grad = half_with_far(flat(cotangent), core_at)
    grad_done_b = cotangent.astype(F32)
    grad_ff_b, grad_hidden_b = hidden_backward(grad_done_b, down_b, kept_b[3])
    grad_mid_b, grad_att_b, grad_mix_b = feed_backward(
        grad_done_b, grad_hidden_b, None, out_b, gain_b2, up_b, kept_b[1]
    )
    grads = split_pieces(grad_mix_b, place)
    late = [half_with_far(flat(x), core_at) for x in (grad_hidden_b, grad_att_b)]
    grads, early = hold(grads, early)
    grads = exchange(grads)
    operands = [y for x in early + [late[0], early_grad, late[1]] for y in x]
    feed_b = feed_grad(place, bits, (0, 1), operands)
    grads, feed_b = hold(grads, feed_b)
    x_order, z_order, y_order = send_orders(bits)
    feed_chains_b = [Chain(unit, order) for unit, order in zip(feed_b, (x_order, z_order))]
    packed_b, packed_slot = attend_back(place, counts_mine, saved_b, grads, chosen_mine)
    packed_slot = exchange(packed_slot)
    part_chain_b = Chain(qkv_grad(place, bits, 0, acts, 0, packed_b), x_order)
    packed_slot, packed_b, _ = stage(feed_chains_b, packed_slot, packed_b, part_chain_b.state)

    grad_packed_slot = assemble_packed(packed_slot, y_first, core_first)
    slot_grad = norm_back(slot_mid, gain_b1, project_back(grad_packed_slot, qkv_b))
    mid_at_slot = jnp.einsum("bcr,brd->bcd", live_hits, grad_mid_b, precision=EXACT)
    grad_done = jnp.where(live[..., None], mid_at_slot + slot_grad, 0.0)
    grad_ff_a, grad_hidden_a = hidden_backward(grad_done, down_a, kept_a[3])
    (grad_hidden_a,) = stage(feed_chains_b, grad_hidden_a)
    (grad_hidden_a,) = meet([part_chain_b], grad_hidden_a)
    grad_mid_a, grad_att_a, grad_mix_a = feed_backward(
        grad_done, grad_hidden_a, router, out_a, gain_a2, up_a, kept_a[1]
    )
    grads = split_pieces(grad_mix_a, place)
    late = [
        half_with_far(flat(x), core_at) for x in (grad_hidden_a, grad_ff_a, grad_att_a)
    ]
    grads = exchange(grads)
    grad_router = jnp.sum(kept_a[0] * grad_mid_a, axis=-1)
    grad_route = jnp.einsum("bc,bcd->d", grad_router, picked, precision=EXACT)
    route = jnp.pad(
        grad_route.reshape(dp_size, 1, narrow), ((0, 0), (0, SPARE - 1), (0, half - narrow))
    )
    operands = [y for x in early_a + late for y in x]
    feed_a = feed_grad(place, bits, (0, 1), operands, route)
    grads, feed_a = stage(feed_chains_b + [part_chain_b], grads, feed_a)
    part_chain_b.step()
    feed_chain_b = merge(feed_chains_b)
    feed_chains_a = [Chain(unit, order) for unit, order in zip(feed_a, (x_order, z_order))]
    packed_a, _ = attend_back(place, counts_mine, saved_a, grads)
    (packed_a,) = meet([part_chain_b], packed_a)
    returned_a = exchange(packed_a)
    part_chain_a = Chain(qkv_grad(place, bits, 2, acts, rows, packed_a), y_order)
    returned_a, packed_b, kept_last, gains = meet(
        [part_chain_a, feed_chain_b],
        returned_a,
        packed_b,
        kept_b[4],
        (gain_a1, gain_a2, gain_b1, gain_b2),
    )
    done_b = kept_b[1] + project(kept_last, down_b)
    gains = lax.dynamic_slice_in_dim(jnp.stack(gains), dp_at * narrow, narrow, axis=1)
    gains = gains.astype(F32)

    grad_packed_a = assemble_packed(returned_a, y_first, core_first)
    res_a = norm_back(picked, gain_a1, project_back(grad_packed_a, qkv_a))
    grad_picked = (
        grad_mid_a + res_a + grad_router[..., None] * route_w.astype(F32) - grad_done
    )
    late_weight, packed_b = hold(qkv_b, packed_b)
    weight_parts = [
        lax.dynamic_slice_in_dim(late_weight, part * width + core_at * half, half, axis=1)
        for part in range(3)
    ]
    shares = [
        sum(dot(piece[part], weight_parts[part], NT) for part in range(3)) for piece in packed_b
    ]
    tail = feed_chains_a + [part_chain_a]
    b_side = [feed_chain_b, part_chain_b]
    for chain in tail:
        chain.step()
    feed_chain_b.step()
    given = swap(jnp.stack([shares[1].astype(BF16), shares[3].astype(BF16)]), "seq", 1)
    act_near = shares[0] + given[0].astype(F32)
    act_far = (shares[2] + given[1].astype(F32)).astype(BF16)
    grad_picked, act_near, act_far, done_b, gains = meet(
        tail + b_side, grad_picked, act_near, act_far, done_b, gains
    )
    part_chain_b.step()
    stage(tail)
    meet([part_chain_b], tail[0].state)
    if not part_chain_b.done:
        part_chain_b.step()
    (act_far,) = stage(tail, act_far)
    act_far = swap(act_far, "seq", 2).astype(F32)
    last = merge(tail)
    for chain in [last] + b_side:
        while not chain.done:
            chain.step()
    def gain_grad(found, weight, gain):
        at = dp_at * narrow
        weight = lax.dynamic_slice_in_dim(weight, at, narrow, axis=0).astype(F32)
        return jnp.sum(found * weight, axis=1) / gain

    near_b, far_b = gather_halves(
        jnp.concatenate([feed_chain_b.state, part_chain_b.state]), y_first
    )

    grad_act_b = jnp.stack(
        [jnp.where(y_first, act_near, act_far), jnp.where(y_first, act_far, act_near)]
    )
    res_b = norm_back(middle, gain_b1, grad_act_b)
    grad_input = grad_mid_b + res_b + scatter(grad_picked)
    qkv_gb, out_gb, up_gb, down_gb = finish(place, OWNERS * narrow, narrow, width, near_b, far_b)
    own = last.state
    gains_b = gain_grad(qkv_gb, qkv_b, gains[2]), gain_grad(up_gb, up_b, gains[3])
    other, gains_b, _ = hold(
        swap(own, "seq", 2), gains_b, (qkv_gb, out_gb, up_gb, down_gb, grad_input)
    )
    near = jnp.stack([jnp.where(y_first, own, other), jnp.where(y_first, other, own)])
    far = swap(near, "seq", 1)
    down_at = OWNERS * narrow + SPARE
    qkv_ga, out_ga, up_ga, down_ga = finish(place, down_at, narrow, width, near, far)
    at = OWNERS * narrow // 2
    route = near[0, at, :narrow].astype(F32) + far[0, at, :narrow].astype(F32)

    return (
        done_b.astype(BF16),
        grad_input,
        route,
        gain_grad(qkv_ga, qkv_a, gains[0]),
        qkv_ga,
        out_ga,
        gain_grad(up_ga, up_a, gains[1]),
        up_ga,
        down_ga,
        gains_b[0],
        qkv_gb,
        out_gb,
        gains_b[1],
        up_gb,
        down_gb,
    )


def solution(mesh):
    tokens, whole, shared = P("dp", "seq", None), P(), P("dp")
    weights = P("dp", None)
    return jax.shard_map(
        per_device,
        mesh=mesh,
        in_specs=(tokens, P("dp", "seq"), P("dp", None)) + (whole,) * 13 + (tokens,),
        out_specs=(tokens, tokens, shared)
        + (shared, weights, weights, shared, weights, weights) * 2,
        check_vma=False,
    )
```
